128 devices in a mesh: yslab: 4 (over x_hi, core), zblock: 32 (over z, x_lo, y).
Axes of the slice: x: 4 (x_hi: 2, x_lo: 2; x = x_hi * 2 + x_lo), y: 4, z: 4, core: 2. Of those that a mesh axis runs over, the one named last changes fastest.
Arguments:
- volume: float32 [512, 512, 512], P('yslab', 'zblock'), may hold values from -6 to 6
- shift_x: int32 [2, 512], replicated, may hold values from -11584 to 11584, as said below
- shift_z: int32 [2, 512], replicated, may hold values from -11584 to 11584, as said below
- mask: int32 [2, 512, 512], P(None, 'yslab', 'zblock'), may hold values from 0 to 1, as said below
- measured: float32 [2, 2, 512, 512], P(None, None, 'yslab', 'zblock'), may hold values from -6 to 6
Outputs:
- corrected: float32 [2, 2, 512, 512], P(None, None, 'yslab', 'zblock')
The draws below stay inside these ranges and needn't reach their ends.
Inputs may be any that keep to these rules, and one draw needn't show every extreme that they name: shift_x holds shifts in units of 1/64 of a cell. shift_z holds shifts in units of 1/64 of a cell. mask[t] is 1 exactly where |q_y(h)| * 512 * a_t <= |q_x(k)| * 512 * b_t with signed frequencies and integers a_t, b_t of 1 to 3, else 0.
All inputs are finite; a program needn't handle non-finite values.
Results may differ from the reference program's by a relative error of at most 0.0001.
Values sent between devices are 32-bit elements; how exact they have to be, the bound alone decides.
No kernel may reach another device: no remote copies, remote signals or barrier semaphores. Data moves between devices by JAX's collectives and lax.ppermute only.
A program may use at most 128 MiB of HBM per device.

```python
import math
import jax
import jax.numpy as jnp
from jax import lax

NX = 512
NZ = 512
TILTS = 2
SUB = 64
NY = 512


def draw_line_shifts(key, length, salt):
    drawn = jax.random.randint(jax.random.fold_in(key, salt), (TILTS, 1), -45, 46)
    flip = jax.random.randint(jax.random.fold_in(key, salt + 2), (1, 1), 0, 2) * 2 - 1
    tilt_index = jnp.arange(TILTS, dtype=jnp.int32)[:, None]
    alternate = jnp.where(jnp.mod(tilt_index, 2) == 0, 1, -1) * flip * 45
    slope = jnp.where(tilt_index < 2, alternate, drawn)
    jitter = jax.random.randint(jax.random.fold_in(key, salt + 1), (TILTS, length), -64, 65)
    first_col = jnp.arange(length, dtype=jnp.int32)[None, :] == 0
    edge = jnp.where(slope > 0, -64, 64)
    jitter = jnp.where(first_col, edge, jitter)
    place = jnp.arange(length, dtype=jnp.int32) - length // 2
    return (slope * place[None, :] + jitter).astype(jnp.int32)


def draw_shift_x(key, part):
    return draw_line_shifts(key, NZ, 11)


def draw_shift_z(key, part):
    return draw_line_shifts(key, NX, 23)


def draw_mask(key, part):
    steep = jax.random.randint(jax.random.fold_in(key, 37), (TILTS, 1, 1), 1, 4)
    flat = jax.random.randint(jax.random.fold_in(key, 41), (TILTS, 1, 1), 1, 4)
    rows_freq = jnp.arange(NY, dtype=jnp.int32)
    cols_freq = jnp.arange(NX, dtype=jnp.int32)
    rows_signed = jnp.abs(jnp.mod(rows_freq + NY // 2, NY) - NY // 2)
    cols_signed = jnp.abs(jnp.mod(cols_freq + NX // 2, NX) - NX // 2)
    inside = rows_signed[None, :, None] * NX * steep <= cols_signed[None, None, :] * NY * flat
    return jnp.where(inside, 1, 0).astype(jnp.int32)


def block_scale(rng, extent, cuts, least, largest):
    loudness = 1.0
    for position, blocks in cuts:
        heights = jax.random.uniform(jax.random.fold_in(jax.random.fold_in(rng, 6), position), (blocks,), jnp.float32, least / len(cuts), largest / len(cuts))
        loudness = loudness * jnp.repeat(jnp.exp(heights), extent[position] // blocks).reshape((-1,) + (1,) * (len(extent) - 1 - position))
    return loudness


def scatter_about(own_key, extent, scale, most, cuts=(), kind=jnp.bfloat16):
    level = block_scale(own_key, extent, cuts, -0.22, 0.18) if cuts else 1.0
    values = jax.random.normal(own_key, extent, jnp.float32) * scale * level
    return jnp.minimum(jnp.maximum(values, -most), most).astype(kind)


def setup_inputs(seed: int = 0) -> dict:
    arg_keys = jax.random.split(jax.random.key(seed), 6)
    volume = scatter_about(arg_keys[0], (NY, NZ, NX), 1.0, 6.0, ((0, 4), (1, 32)), jnp.float32)
    shift_x = draw_shift_x(jax.random.fold_in(arg_keys[5], 71), 0)
    shift_z = draw_shift_z(jax.random.fold_in(arg_keys[5], 71), 0)
    mask = draw_mask(jax.random.fold_in(arg_keys[5], 71), 0)
    measured = scatter_about(arg_keys[4], (2, TILTS, NY, NX), 1.0, 6.0, ((2, 4), (3, 32)), jnp.float32)
    return {"volume": volume, "shift_x": shift_x, "shift_z": shift_z, "mask": mask, "measured": measured}


def ramp_pair(shifts, length):
    freq = jnp.arange(length, dtype=jnp.int32)
    signed = jnp.mod(freq + length // 2, length) - length // 2
    turns = jnp.mod(shifts[..., None] * signed, SUB * length).astype(jnp.float32)
    angle = 2.0 * math.pi / (SUB * length) * turns
    return (jnp.cos(angle), jnp.sin(angle))

def reference(volume, shift_x, shift_z, mask, measured):
    results = []
    volume_spec = jnp.fft.fft(volume, axis=2)
    for tilt in range(TILTS):
        cos_x, sin_x = ramp_pair(shift_x[tilt], NX)
        phase_x = cos_x - 1j * sin_x
        first = jnp.real(jnp.fft.ifft(volume_spec * phase_x[None], axis=2))
        cos_z, sin_z = ramp_pair(shift_z[tilt], NZ)
        phase_z = jnp.transpose(cos_z - 1j * sin_z)
        second = jnp.real(jnp.fft.ifft(jnp.fft.fft(first, axis=1) * phase_z[None], axis=1))
        third = jnp.fft.fft(second, axis=2) * phase_x[None]
        line = lax.optimization_barrier(jnp.sum(third, axis=1)) / math.sqrt(NZ * NX)
        results.append(jnp.fft.fft(line, axis=0) / math.sqrt(NY))
    spectrum = jnp.stack(results)
    spectrum = jnp.stack([jnp.real(spectrum), jnp.imag(spectrum)]).astype(jnp.float32)
    weight = mask.astype(jnp.float32)[None]
    return spectrum + weight * (measured - spectrum)
```

```python
import math

import jax
import jax.numpy as jnp
from jax import lax
from jax.sharding import PartitionSpec as P

SUB = 64


HIGH = lax.Precision.HIGHEST


def wave_pair(first, second, length):
    turns = jnp.mod(first[:, None] * second[None, :], length).astype(jnp.float32)
    angle = 2.0 * math.pi / length * turns
    return (jnp.cos(angle), jnp.sin(angle))


def ramp_pair(shifts, length):
    freq = jnp.arange(length, dtype=jnp.int32)
    signed = jnp.mod(freq + length // 2, length) - length // 2
    turns = jnp.mod(shifts[..., None] * signed, SUB * length).astype(jnp.float32)
    angle = 2.0 * math.pi / (SUB * length) * turns
    return (jnp.cos(angle), jnp.sin(angle))


def shear_back(real_part, imag_part, ramp_cos, ramp_sin, wave_cos, wave_sin):
    turned_re = real_part * ramp_cos + imag_part * ramp_sin
    turned_im = imag_part * ramp_cos - real_part * ramp_sin
    length = wave_cos.shape[0]
    return (
        jnp.matmul(turned_re, wave_cos, precision=HIGH)
        - jnp.matmul(turned_im, wave_sin, precision=HIGH)
    ) / length


def on_device(volume, shift_x, shift_z, mask, measured):
    zparts = lax.axis_size("zblock")
    zindex = lax.axis_index("zblock")
    yindex = lax.axis_index("yslab")
    ydev, zdev, width = volume.shape
    depth = zdev * zparts
    xdev = width // zparts
    zstart = zindex * zdev
    xstart = zindex * xdev
    xfreq = jnp.arange(width, dtype=jnp.int32)
    zfreq = jnp.arange(depth, dtype=jnp.int32)
    xcos, xsin = wave_pair(xfreq, xfreq, width)
    zcos, zsin = wave_pair(zfreq, zfreq, depth)
    scale = 1.0 / math.sqrt(depth * width)

    def depth_shear(columns, column_cos, column_sin):
        depth_re = jnp.einsum("tyzx,zk->tyxk", columns, zcos, precision=HIGH)
        depth_im = -jnp.einsum("tyzx,zk->tyxk", columns, zsin, precision=HIGH)
        return shear_back(depth_re, depth_im, column_cos, column_sin, zcos, zsin)

    volume_re = jnp.matmul(volume, xcos, precision=HIGH)
    volume_im = -jnp.matmul(volume, xsin, precision=HIGH)

    def project(first_shifts, second_shifts):
        local_shift = lax.dynamic_slice_in_dim(first_shifts, zstart, zdev, 1)
        near_cos, near_sin = ramp_pair(local_shift, width)
        first = shear_back(
            volume_re[None], volume_im[None], near_cos[:, None], near_sin[:, None], xcos, xsin
        )
        column_shift = lax.dynamic_slice_in_dim(second_shifts, xstart, xdev, 1)
        column_cos, column_sin = ramp_pair(column_shift, depth)
        second = depth_shear(
            lax.all_to_all(first, "zblock", split_axis=3, concat_axis=2, tiled=True),
            column_cos[:, None],
            column_sin[:, None],
        )
        blocks = lax.all_to_all(second, "zblock", split_axis=3, concat_axis=2, tiled=True)
        line_re = jnp.einsum("tyxz,xk->tyzk", blocks, xcos, precision=HIGH)
        line_im = -jnp.einsum("tyxz,xk->tyzk", blocks, xsin, precision=HIGH)
        part_re = jnp.sum(line_re * near_cos[:, None] + line_im * near_sin[:, None], axis=2)
        part_im = jnp.sum(line_im * near_cos[:, None] - line_re * near_sin[:, None], axis=2)
        return jnp.stack((part_re[0], part_im[0])) * scale

    pieces = jnp.stack(
        [
            project(shift_x[tilt : tilt + 1], shift_z[tilt : tilt + 1])
            for tilt in range(shift_x.shape[0])
        ]
    )
    tilts = pieces.shape[0]
    kdev = width // zparts
    pieces = pieces.reshape(tilts, 2, ydev, zparts, kdev)
    pieces = jnp.moveaxis(pieces, 3, 0)
    pieces = lax.all_to_all(pieces, "zblock", 0, 0, tiled=True)
    lines = jnp.sum(pieces, axis=0)
    spec_re = lines[:, 0]
    spec_im = lines[:, 1]
    yparts = lax.axis_size("yslab")
    rows_all = ydev * yparts
    ylocal = jnp.arange(ydev, dtype=jnp.int32) + yindex * ydev
    kfreq = jnp.arange(rows_all, dtype=jnp.int32)
    wave_cos, wave_sin = wave_pair(kfreq, ylocal, rows_all)
    term_re = jnp.einsum("ky,tyx->ktx", wave_cos, spec_re, precision=HIGH) + jnp.einsum(
        "ky,tyx->ktx", wave_sin, spec_im, precision=HIGH
    )
    term_im = jnp.einsum("ky,tyx->ktx", wave_cos, spec_im, precision=HIGH) - jnp.einsum(
        "ky,tyx->ktx", wave_sin, spec_re, precision=HIGH
    )
    terms = jnp.stack((term_re, term_im), axis=1) / math.sqrt(rows_all)
    terms = terms.reshape((yparts, ydev) + terms.shape[1:])
    terms = lax.all_to_all(terms, "yslab", 0, 0, tiled=True)
    gathered = jnp.sum(terms, axis=0)
    spectrum = jnp.transpose(gathered, (1, 2, 0, 3))
    weight = mask.astype(jnp.float32)[None]
    return spectrum + weight * (measured - spectrum)


def solution(mesh):
    in_specs = (
        P("yslab", "zblock", None),
        P(),
        P(),
        P(None, "yslab", "zblock"),
        P(None, None, "yslab", "zblock"),
    )
    out_specs = P(None, None, "yslab", "zblock")
    return jax.shard_map(
        on_device, mesh=mesh, in_specs=in_specs, out_specs=out_specs, check_vma=False
    )
```

```python
import math

import jax
import jax.numpy as jnp
from jax import lax
from jax.sharding import PartitionSpec as P

SUB = 64


HIGH = lax.Precision.HIGH


def wave_pair(first, second, length):
    turns = jnp.mod(first[:, None] * second[None, :], length).astype(jnp.float32)
    angle = 2.0 * math.pi / length * turns
    return (jnp.cos(angle), jnp.sin(angle))


def ramp_pair(shifts, length):
    freq = jnp.arange(length, dtype=jnp.int32)
    signed = jnp.mod(freq + length // 2, length) - length // 2
    turns = jnp.mod(shifts[..., None] * signed, SUB * length).astype(jnp.float32)
    angle = 2.0 * math.pi / (SUB * length) * turns
    return (jnp.cos(angle), jnp.sin(angle))


def shear_back(real_part, imag_part, ramp_cos, ramp_sin, wave_cos, wave_sin):
    turned_re = real_part * ramp_cos + imag_part * ramp_sin
    turned_im = imag_part * ramp_cos - real_part * ramp_sin
    length = wave_cos.shape[0]
    return (
        jnp.matmul(turned_re, wave_cos, precision=HIGH)
        - jnp.matmul(turned_im, wave_sin, precision=HIGH)
    ) / length


def on_device(volume, shift_x, shift_z, mask, measured):
    zparts = lax.axis_size("zblock")
    zindex = lax.axis_index("zblock")
    yindex = lax.axis_index("yslab")
    ydev, zdev, width = volume.shape
    depth = zdev * zparts
    xdev = width // zparts
    zstart = zindex * zdev
    xstart = zindex * xdev
    xfreq = jnp.arange(width, dtype=jnp.int32)
    zfreq = jnp.arange(depth, dtype=jnp.int32)
    xcos, xsin = wave_pair(xfreq, xfreq, width)
    zcos, zsin = wave_pair(zfreq, zfreq, depth)
    scale = 1.0 / math.sqrt(depth * width)

    def depth_shear(columns, column_cos, column_sin):
        depth_re = jnp.einsum("tyzx,zk->tyxk", columns, zcos, precision=HIGH)
        depth_im = -jnp.einsum("tyzx,zk->tyxk", columns, zsin, precision=HIGH)
        return shear_back(depth_re, depth_im, column_cos, column_sin, zcos, zsin)

    volume_re = jnp.matmul(volume, xcos, precision=HIGH)
    volume_im = -jnp.matmul(volume, xsin, precision=HIGH)

    def project(first_shifts, second_shifts):
        local_shift = lax.dynamic_slice_in_dim(first_shifts, zstart, zdev, 1)
        near_cos, near_sin = ramp_pair(local_shift, width)
        first = shear_back(
            volume_re[None], volume_im[None], near_cos[:, None], near_sin[:, None], xcos, xsin
        )
        column_shift = lax.dynamic_slice_in_dim(second_shifts, xstart, xdev, 1)
        column_cos, column_sin = ramp_pair(column_shift, depth)
        second = depth_shear(
            lax.all_to_all(first, "zblock", split_axis=3, concat_axis=2, tiled=True),
            column_cos[:, None],
            column_sin[:, None],
        )
        blocks = lax.all_to_all(second, "zblock", split_axis=3, concat_axis=2, tiled=True)
        line_re = jnp.einsum("tyxz,xk->tyzk", blocks, xcos, precision=HIGH)
        line_im = -jnp.einsum("tyxz,xk->tyzk", blocks, xsin, precision=HIGH)
        part_re = jnp.sum(line_re * near_cos[:, None] + line_im * near_sin[:, None], axis=2)
        part_im = jnp.sum(line_im * near_cos[:, None] - line_re * near_sin[:, None], axis=2)
        return jnp.stack((part_re[0], part_im[0])) * scale

    pieces = jnp.stack(
        [
            project(shift_x[tilt : tilt + 1], shift_z[tilt : tilt + 1])
            for tilt in range(shift_x.shape[0])
        ]
    )
    tilts = pieces.shape[0]
    kdev = width // zparts
    pieces = pieces.reshape(tilts, 2, ydev, zparts, kdev)
    pieces = jnp.moveaxis(pieces, 3, 0)
    pieces = lax.all_to_all(pieces, "zblock", 0, 0, tiled=True)
    lines = jnp.sum(pieces, axis=0)
    spec_re = lines[:, 0]
    spec_im = lines[:, 1]
    yparts = lax.axis_size("yslab")
    rows_all = ydev * yparts
    ylocal = jnp.arange(ydev, dtype=jnp.int32) + yindex * ydev
    kfreq = jnp.arange(rows_all, dtype=jnp.int32)
    wave_cos, wave_sin = wave_pair(kfreq, ylocal, rows_all)
    term_re = jnp.einsum("ky,tyx->ktx", wave_cos, spec_re, precision=HIGH) + jnp.einsum(
        "ky,tyx->ktx", wave_sin, spec_im, precision=HIGH
    )
    term_im = jnp.einsum("ky,tyx->ktx", wave_cos, spec_im, precision=HIGH) - jnp.einsum(
        "ky,tyx->ktx", wave_sin, spec_re, precision=HIGH
    )
    terms = jnp.stack((term_re, term_im), axis=1) / math.sqrt(rows_all)
    terms = terms.reshape((yparts, ydev) + terms.shape[1:])
    terms = lax.all_to_all(terms, "yslab", 0, 0, tiled=True)
    gathered = jnp.sum(terms, axis=0)
    spectrum = jnp.transpose(gathered, (1, 2, 0, 3))
    weight = mask.astype(jnp.float32)[None]
    return spectrum + weight * (measured - spectrum)


def solution(mesh):
    in_specs = (
        P("yslab", "zblock", None),
        P(),
        P(),
        P(None, "yslab", "zblock"),
        P(None, None, "yslab", "zblock"),
    )
    out_specs = P(None, None, "yslab", "zblock")
    return jax.shard_map(
        on_device, mesh=mesh, in_specs=in_specs, out_specs=out_specs, check_vma=False
    )
```

```python
import math

import jax
import jax.numpy as jnp
from jax import lax
from jax.sharding import PartitionSpec as P

SUB = 64


HIGH = lax.Precision.HIGH


def wave_pair(first, second, length):
    turns = jnp.mod(first[:, None] * second[None, :], length).astype(jnp.float32)
    angle = 2.0 * math.pi / length * turns
    return (jnp.cos(angle), jnp.sin(angle))


def ramp_pair(shifts, length):
    freq = jnp.arange(length, dtype=jnp.int32)
    signed = jnp.mod(freq + length // 2, length) - length // 2
    turns = jnp.mod(shifts[..., None] * signed, SUB * length).astype(jnp.float32)
    angle = 2.0 * math.pi / (SUB * length) * turns
    return (jnp.cos(angle), jnp.sin(angle))


def signed_turns(shifts, freq, length):
    signed = jnp.mod(freq + length // 2, length) - length // 2
    turns = jnp.mod(shifts[..., None] * signed, SUB * length).astype(jnp.float32)
    angle = 2.0 * math.pi / (SUB * length) * turns
    return (jnp.cos(angle), jnp.sin(angle))


def packed_forward(length):
    half = length // 2
    pos = jnp.arange(length, dtype=jnp.int32)
    freq = jnp.arange(half, dtype=jnp.int32)
    wc, ws = wave_pair(pos, freq, length)
    alt = jnp.where(pos % 2 == 0, 1.0, -1.0).astype(jnp.float32)
    im_cols = jnp.concatenate([alt[:, None], -ws[:, 1:]], axis=1)
    return jnp.concatenate([wc, im_cols], axis=1)


def packed_inverse(length):
    half = length // 2
    pos = jnp.arange(length, dtype=jnp.int32)
    freq = jnp.arange(half, dtype=jnp.int32)
    wc, ws = wave_pair(freq, pos, length)
    alt = jnp.where(pos % 2 == 0, 1.0, -1.0).astype(jnp.float32)
    weight = jnp.where(freq == 0, 1.0, 2.0).astype(jnp.float32)[:, None]
    re_rows = wc * weight
    im_rows = jnp.concatenate([alt[None, :], -2.0 * ws[1:]], axis=0)
    return jnp.concatenate([re_rows, im_rows], axis=0) / length


def packed_phase(shifts, length):
    half = length // 2
    freq = jnp.arange(half + 1, dtype=jnp.int32)
    cos_k, sin_k = signed_turns(shifts, freq, length)
    zero = jnp.zeros_like(sin_k[..., :1])
    scale_a = jnp.concatenate([cos_k[..., :half], cos_k[..., half:], cos_k[..., 1:half]], axis=-1)
    scale_b = jnp.concatenate([zero, sin_k[..., 1:half], zero, -sin_k[..., 1:half]], axis=-1)
    return scale_a, scale_b


def turn(spec, scale_a, scale_b):
    half = spec.shape[-1] // 2
    return spec * scale_a + jnp.roll(spec, half, axis=-1) * scale_b


def on_device(volume, shift_x, shift_z, mask, measured):
    zparts = lax.axis_size("zblock")
    zindex = lax.axis_index("zblock")
    yindex = lax.axis_index("yslab")
    ydev, zdev, width = volume.shape
    depth = zdev * zparts
    xdev = width // zparts
    zstart = zindex * zdev
    xstart = zindex * xdev
    tilts = shift_x.shape[0]
    scale = 1.0 / math.sqrt(depth * width)

    fx = packed_forward(width)
    gx = packed_inverse(width)
    fz = packed_forward(depth)
    gz = packed_inverse(depth)
    xfreq = jnp.arange(width, dtype=jnp.int32)
    xlocal = jnp.arange(xdev, dtype=jnp.int32) + xstart
    line_wc, line_ws = wave_pair(xlocal, xfreq, width)

    rows = volume.reshape(ydev * zdev, width)
    spec_x = jnp.matmul(rows, fx, precision=HIGH).reshape(ydev, zdev, width)

    partial = []
    for tilt in range(tilts):
        local_shift = lax.dynamic_slice_in_dim(shift_x[tilt], zstart, zdev, 0)
        near_a, near_b = packed_phase(local_shift, width)
        turned = turn(spec_x, near_a[None], near_b[None])
        first = jnp.matmul(turned.reshape(ydev * zdev, width), gx, precision=HIGH)
        first = first.reshape(ydev, zdev, width)
        columns = lax.all_to_all(first, "zblock", split_axis=2, concat_axis=1, tiled=True)
        columns = jnp.transpose(columns, (0, 2, 1))
        spec_z = jnp.matmul(columns.reshape(ydev * xdev, depth), fz, precision=HIGH)
        column_shift = lax.dynamic_slice_in_dim(shift_z[tilt], xstart, xdev, 0)
        col_a, col_b = packed_phase(column_shift, depth)
        turned_z = turn(spec_z.reshape(ydev, xdev, depth), col_a[None], col_b[None])
        second = jnp.matmul(turned_z.reshape(ydev * xdev, depth), gz, precision=HIGH)
        second = second.reshape(ydev, xdev * depth)
        ph_c, ph_s = ramp_pair(shift_x[tilt], width)
        m_re = line_wc[:, None, :] * ph_c[None] - line_ws[:, None, :] * ph_s[None]
        m_im = -(line_wc[:, None, :] * ph_s[None] + line_ws[:, None, :] * ph_c[None])
        line_re = jnp.matmul(second, m_re.reshape(xdev * depth, width), precision=HIGH)
        line_im = jnp.matmul(second, m_im.reshape(xdev * depth, width), precision=HIGH)
        partial.append(jnp.stack((line_re, line_im)) * scale)

    pieces = jnp.stack(partial)
    kdev = width // zparts
    pieces = pieces.reshape(tilts, 2, ydev, zparts, kdev)
    pieces = jnp.moveaxis(pieces, 3, 0)
    pieces = lax.all_to_all(pieces, "zblock", 0, 0, tiled=True)
    lines = jnp.sum(pieces, axis=0)
    spec_re = lines[:, 0]
    spec_im = lines[:, 1]
    yparts = lax.axis_size("yslab")
    rows_all = ydev * yparts
    ylocal = jnp.arange(ydev, dtype=jnp.int32) + yindex * ydev
    kfreq = jnp.arange(rows_all, dtype=jnp.int32)
    wave_cos, wave_sin = wave_pair(kfreq, ylocal, rows_all)
    term_re = jnp.einsum("ky,tyx->ktx", wave_cos, spec_re, precision=HIGH) + jnp.einsum(
        "ky,tyx->ktx", wave_sin, spec_im, precision=HIGH
    )
    term_im = jnp.einsum("ky,tyx->ktx", wave_cos, spec_im, precision=HIGH) - jnp.einsum(
        "ky,tyx->ktx", wave_sin, spec_re, precision=HIGH
    )
    terms = jnp.stack((term_re, term_im), axis=1) / math.sqrt(rows_all)
    terms = terms.reshape((yparts, ydev) + terms.shape[1:])
    terms = lax.all_to_all(terms, "yslab", 0, 0, tiled=True)
    gathered = jnp.sum(terms, axis=0)
    spectrum = jnp.transpose(gathered, (1, 2, 0, 3))
    weight = mask.astype(jnp.float32)[None]
    return spectrum + weight * (measured - spectrum)


def solution(mesh):
    in_specs = (
        P("yslab", "zblock", None),
        P(),
        P(),
        P(None, "yslab", "zblock"),
        P(None, None, "yslab", "zblock"),
    )
    out_specs = P(None, None, "yslab", "zblock")
    return jax.shard_map(
        on_device, mesh=mesh, in_specs=in_specs, out_specs=out_specs, check_vma=False
    )
```

```python
import math

import jax
import jax.numpy as jnp
from jax import lax
from jax.sharding import PartitionSpec as P

SUB = 64


HIGH = lax.Precision.HIGH


def wave_pair(first, second, length):
    turns = jnp.mod(first[:, None] * second[None, :], length).astype(jnp.float32)
    angle = 2.0 * math.pi / length * turns
    return (jnp.cos(angle), jnp.sin(angle))


def ramp_pair(shifts, length):
    freq = jnp.arange(length, dtype=jnp.int32)
    signed = jnp.mod(freq + length // 2, length) - length // 2
    turns = jnp.mod(shifts[..., None] * signed, SUB * length).astype(jnp.float32)
    angle = 2.0 * math.pi / (SUB * length) * turns
    return (jnp.cos(angle), jnp.sin(angle))


def signed_turns(shifts, freq, length):
    signed = jnp.mod(freq + length // 2, length) - length // 2
    turns = jnp.mod(shifts[..., None] * signed, SUB * length).astype(jnp.float32)
    angle = 2.0 * math.pi / (SUB * length) * turns
    return (jnp.cos(angle), jnp.sin(angle))


def packed_forward(length):
    half = length // 2
    pos = jnp.arange(length, dtype=jnp.int32)
    freq = jnp.arange(half, dtype=jnp.int32)
    wc, ws = wave_pair(pos, freq, length)
    alt = jnp.where(pos % 2 == 0, 1.0, -1.0).astype(jnp.float32)
    im_cols = jnp.concatenate([alt[:, None], -ws[:, 1:]], axis=1)
    return jnp.concatenate([wc, im_cols], axis=1)


def packed_inverse(length):
    half = length // 2
    pos = jnp.arange(length, dtype=jnp.int32)
    freq = jnp.arange(half, dtype=jnp.int32)
    wc, ws = wave_pair(freq, pos, length)
    alt = jnp.where(pos % 2 == 0, 1.0, -1.0).astype(jnp.float32)
    weight = jnp.where(freq == 0, 1.0, 2.0).astype(jnp.float32)[:, None]
    re_rows = wc * weight
    im_rows = jnp.concatenate([alt[None, :], -2.0 * ws[1:]], axis=0)
    return jnp.concatenate([re_rows, im_rows], axis=0) / length


def packed_phase(shifts, length):
    half = length // 2
    freq = jnp.arange(half + 1, dtype=jnp.int32)
    cos_k, sin_k = signed_turns(shifts, freq, length)
    zero = jnp.zeros_like(sin_k[..., :1])
    scale_a = jnp.concatenate([cos_k[..., :half], cos_k[..., half:], cos_k[..., 1:half]], axis=-1)
    scale_b = jnp.concatenate([zero, sin_k[..., 1:half], zero, -sin_k[..., 1:half]], axis=-1)
    return scale_a, scale_b


def turn(spec, scale_a, scale_b):
    half = spec.shape[-1] // 2
    low, high = spec[..., :half], spec[..., half:]
    out_low = low * scale_a[..., :half] + high * scale_b[..., :half]
    out_high = high * scale_a[..., half:] + low * scale_b[..., half:]
    return jnp.concatenate([out_low, out_high], axis=-1)


def on_device(volume, shift_x, shift_z, mask, measured):
    zparts = lax.axis_size("zblock")
    zindex = lax.axis_index("zblock")
    yindex = lax.axis_index("yslab")
    ydev, zdev, width = volume.shape
    depth = zdev * zparts
    xdev = width // zparts
    zstart = zindex * zdev
    xstart = zindex * xdev
    tilts = shift_x.shape[0]
    scale = 1.0 / math.sqrt(depth * width)
    half = width // 2

    fx = packed_forward(width)
    gx = packed_inverse(width)
    fz = packed_forward(depth)
    gz = packed_inverse(depth)

    xfreq = jnp.arange(width, dtype=jnp.int32)
    xlocal = jnp.arange(xdev, dtype=jnp.int32) + xstart
    line_wc, line_ws = wave_pair(xlocal, xfreq, width)

    rows = volume.reshape(ydev * zdev, width)
    spec_x = jnp.matmul(rows, fx, precision=HIGH).reshape(ydev, zdev, width)

    partial = []
    for tilt in range(tilts):
        local_shift = lax.dynamic_slice_in_dim(shift_x[tilt], zstart, zdev, 0)
        near_a, near_b = packed_phase(local_shift, width)
        turned = turn(spec_x, near_a[None], near_b[None])
        first = jnp.matmul(turned.reshape(ydev * zdev, width), gx, precision=HIGH)
        first = first.reshape(ydev, zdev, width)
        columns = lax.all_to_all(first, "zblock", split_axis=2, concat_axis=1, tiled=True)
        columns = jnp.transpose(columns, (0, 2, 1))
        spec_z = jnp.matmul(columns.reshape(ydev * xdev, depth), fz, precision=HIGH)
        column_shift = lax.dynamic_slice_in_dim(shift_z[tilt], xstart, xdev, 0)
        col_a, col_b = packed_phase(column_shift, depth)
        turned_z = turn(spec_z.reshape(ydev, xdev, depth), col_a[None], col_b[None])
        ph_c, ph_s = ramp_pair(shift_x[tilt], width)
        depth_to_line = jnp.matmul(gz, jnp.concatenate([ph_c, ph_s], axis=1), precision=HIGH)
        mixed = jnp.matmul(turned_z.reshape(ydev * xdev, depth), depth_to_line, precision=HIGH)
        mixed = mixed.reshape(ydev, xdev, 2 * width)
        mix_c, mix_s = mixed[..., :width], mixed[..., width:]
        full_re = jnp.sum(line_wc[None] * mix_c - line_ws[None] * mix_s, axis=1)
        full_im = -jnp.sum(line_wc[None] * mix_s + line_ws[None] * mix_c, axis=1)
        partial.append(jnp.stack((full_re, full_im)) * scale)

    pieces = jnp.stack(partial)
    kdev = width // zparts
    pieces = pieces.reshape(tilts, 2, ydev, zparts, kdev)
    pieces = jnp.moveaxis(pieces, 3, 0)
    pieces = lax.all_to_all(pieces, "zblock", 0, 0, tiled=True)
    lines = jnp.sum(pieces, axis=0)
    spec_re = lines[:, 0]
    spec_im = lines[:, 1]
    yparts = lax.axis_size("yslab")
    rows_all = ydev * yparts
    ylocal = jnp.arange(ydev, dtype=jnp.int32) + yindex * ydev
    kfreq = jnp.arange(rows_all, dtype=jnp.int32)
    wave_cos, wave_sin = wave_pair(kfreq, ylocal, rows_all)
    term_re = jnp.einsum("ky,tyx->ktx", wave_cos, spec_re, precision=HIGH) + jnp.einsum(
        "ky,tyx->ktx", wave_sin, spec_im, precision=HIGH
    )
    term_im = jnp.einsum("ky,tyx->ktx", wave_cos, spec_im, precision=HIGH) - jnp.einsum(
        "ky,tyx->ktx", wave_sin, spec_re, precision=HIGH
    )
    terms = jnp.stack((term_re, term_im), axis=1) / math.sqrt(rows_all)
    terms = terms.reshape((yparts, ydev) + terms.shape[1:])
    terms = lax.all_to_all(terms, "yslab", 0, 0, tiled=True)
    gathered = jnp.sum(terms, axis=0)
    spectrum = jnp.transpose(gathered, (1, 2, 0, 3))
    weight = mask.astype(jnp.float32)[None]
    return spectrum + weight * (measured - spectrum)


def solution(mesh):
    in_specs = (
        P("yslab", "zblock", None),
        P(),
        P(),
        P(None, "yslab", "zblock"),
        P(None, None, "yslab", "zblock"),
    )
    out_specs = P(None, None, "yslab", "zblock")
    return jax.shard_map(
        on_device, mesh=mesh, in_specs=in_specs, out_specs=out_specs, check_vma=False
    )
```

```python
import math

import jax
import jax.numpy as jnp
from jax import lax
from jax.sharding import PartitionSpec as P

SUB = 64


HIGH = lax.Precision.HIGH


def wave_pair(first, second, length):
    turns = jnp.mod(first[:, None] * second[None, :], length).astype(jnp.float32)
    angle = 2.0 * math.pi / length * turns
    return (jnp.cos(angle), jnp.sin(angle))


def ramp_pair(shifts, length):
    freq = jnp.arange(length, dtype=jnp.int32)
    signed = jnp.mod(freq + length // 2, length) - length // 2
    turns = jnp.mod(shifts[..., None] * signed, SUB * length).astype(jnp.float32)
    angle = 2.0 * math.pi / (SUB * length) * turns
    return (jnp.cos(angle), jnp.sin(angle))


def signed_turns(shifts, freq, length):
    signed = jnp.mod(freq + length // 2, length) - length // 2
    turns = jnp.mod(shifts[..., None] * signed, SUB * length).astype(jnp.float32)
    angle = 2.0 * math.pi / (SUB * length) * turns
    return (jnp.cos(angle), jnp.sin(angle))


def packed_forward(length):
    half = length // 2
    pos = jnp.arange(length, dtype=jnp.int32)
    freq = jnp.arange(half, dtype=jnp.int32)
    wc, ws = wave_pair(pos, freq, length)
    alt = jnp.where(pos % 2 == 0, 1.0, -1.0).astype(jnp.float32)
    im_cols = jnp.concatenate([alt[:, None], -ws[:, 1:]], axis=1)
    return jnp.concatenate([wc, im_cols], axis=1)


def packed_inverse(length):
    half = length // 2
    pos = jnp.arange(length, dtype=jnp.int32)
    freq = jnp.arange(half, dtype=jnp.int32)
    wc, ws = wave_pair(freq, pos, length)
    alt = jnp.where(pos % 2 == 0, 1.0, -1.0).astype(jnp.float32)
    weight = jnp.where(freq == 0, 1.0, 2.0).astype(jnp.float32)[:, None]
    re_rows = wc * weight
    im_rows = jnp.concatenate([alt[None, :], -2.0 * ws[1:]], axis=0)
    return jnp.concatenate([re_rows, im_rows], axis=0) / length


def packed_phase(shifts, length):
    half = length // 2
    freq = jnp.arange(half + 1, dtype=jnp.int32)
    cos_k, sin_k = signed_turns(shifts, freq, length)
    zero = jnp.zeros_like(sin_k[..., :1])
    scale_a = jnp.concatenate([cos_k[..., :half], cos_k[..., half:], cos_k[..., 1:half]], axis=-1)
    scale_b = jnp.concatenate([zero, sin_k[..., 1:half], zero, -sin_k[..., 1:half]], axis=-1)
    return scale_a, scale_b


def turn(spec, scale_a, scale_b):
    half = spec.shape[-1] // 2
    low, high = spec[..., :half], spec[..., half:]
    out_low = low * scale_a[..., :half] + high * scale_b[..., :half]
    out_high = high * scale_a[..., half:] + low * scale_b[..., half:]
    return jnp.concatenate([out_low, out_high], axis=-1)


def on_device(volume, shift_x, shift_z, mask, measured):
    zparts = lax.axis_size("zblock")
    zindex = lax.axis_index("zblock")
    yindex = lax.axis_index("yslab")
    ydev, zdev, width = volume.shape
    depth = zdev * zparts
    xdev = width // zparts
    zstart = zindex * zdev
    xstart = zindex * xdev
    tilts = shift_x.shape[0]
    scale = 1.0 / math.sqrt(depth * width)
    half = width // 2

    fx = packed_forward(width)
    gx = packed_inverse(width)
    fz = packed_forward(depth)
    gz = packed_inverse(depth)

    xfreq = jnp.arange(width, dtype=jnp.int32)
    xlocal = jnp.arange(xdev, dtype=jnp.int32) + xstart
    line_wc, line_ws = wave_pair(xlocal, xfreq, width)

    rows = volume.reshape(ydev * zdev, width)
    spec_x = jnp.matmul(rows, fx, precision=HIGH).reshape(ydev, zdev, width)

    chunks = 2
    ychunk = ydev // chunks
    kdev = width // zparts
    lines = []
    for tilt in range(tilts):
        local_shift = lax.dynamic_slice_in_dim(shift_x[tilt], zstart, zdev, 0)
        near_a, near_b = packed_phase(local_shift, width)
        column_shift = lax.dynamic_slice_in_dim(shift_z[tilt], xstart, xdev, 0)
        col_a, col_b = packed_phase(column_shift, depth)
        ph_c, ph_s = ramp_pair(shift_x[tilt], width)
        depth_to_line = jnp.matmul(gz, jnp.concatenate([ph_c, ph_s], axis=1), precision=HIGH)
        partial = []
        for part in range(chunks):
            spec_part = spec_x[part * ychunk : (part + 1) * ychunk]
            turned = turn(spec_part, near_a[None], near_b[None])
            first = jnp.matmul(turned.reshape(ychunk * zdev, width), gx, precision=HIGH)
            first = first.reshape(ychunk, zdev, width)
            columns = lax.all_to_all(first, "zblock", split_axis=2, concat_axis=1, tiled=True)
            columns = jnp.transpose(columns, (0, 2, 1))
            spec_z = jnp.matmul(columns.reshape(ychunk * xdev, depth), fz, precision=HIGH)
            turned_z = turn(spec_z.reshape(ychunk, xdev, depth), col_a[None], col_b[None])
            mixed = jnp.matmul(turned_z.reshape(ychunk * xdev, depth), depth_to_line, precision=HIGH)
            mixed = mixed.reshape(ychunk, xdev, 2 * width)
            mix_c, mix_s = mixed[..., :width], mixed[..., width:]
            full_re = jnp.sum(line_wc[None] * mix_c - line_ws[None] * mix_s, axis=1)
            full_im = -jnp.sum(line_wc[None] * mix_s + line_ws[None] * mix_c, axis=1)
            partial.append(jnp.stack((full_re, full_im)) * scale)
        pieces = jnp.concatenate(partial, axis=1)
        pieces = pieces.reshape(2, ydev, zparts, kdev)
        pieces = jnp.moveaxis(pieces, 2, 0)
        pieces = lax.all_to_all(pieces, "zblock", 0, 0, tiled=True)
        lines.append(jnp.sum(pieces, axis=0))
    lines = jnp.stack(lines)
    spec_re = lines[:, 0]
    spec_im = lines[:, 1]
    yparts = lax.axis_size("yslab")
    rows_all = ydev * yparts
    ylocal = jnp.arange(ydev, dtype=jnp.int32) + yindex * ydev
    kfreq = jnp.arange(rows_all, dtype=jnp.int32)
    wave_cos, wave_sin = wave_pair(kfreq, ylocal, rows_all)
    term_re = jnp.einsum("ky,tyx->ktx", wave_cos, spec_re, precision=HIGH) + jnp.einsum(
        "ky,tyx->ktx", wave_sin, spec_im, precision=HIGH
    )
    term_im = jnp.einsum("ky,tyx->ktx", wave_cos, spec_im, precision=HIGH) - jnp.einsum(
        "ky,tyx->ktx", wave_sin, spec_re, precision=HIGH
    )
    terms = jnp.stack((term_re, term_im), axis=1) / math.sqrt(rows_all)
    terms = terms.reshape((yparts, ydev) + terms.shape[1:])
    terms = lax.all_to_all(terms, "yslab", 0, 0, tiled=True)
    gathered = jnp.sum(terms, axis=0)
    spectrum = jnp.transpose(gathered, (1, 2, 0, 3))
    weight = mask.astype(jnp.float32)[None]
    return spectrum + weight * (measured - spectrum)


def solution(mesh):
    in_specs = (
        P("yslab", "zblock", None),
        P(),
        P(),
        P(None, "yslab", "zblock"),
        P(None, None, "yslab", "zblock"),
    )
    out_specs = P(None, None, "yslab", "zblock")
    return jax.shard_map(
        on_device, mesh=mesh, in_specs=in_specs, out_specs=out_specs, check_vma=False
    )
```

```python
import math
import os

import jax
import jax.numpy as jnp
from jax import lax
from jax.experimental import pallas as pl
from jax.sharding import PartitionSpec as P

SUB = 64


HIGH = lax.Precision.HIGH
INTERPRET = os.environ.get("SOL_INTERPRET") == "1"
YBLOCK = 32


def split_bf16(value):
    high = value.astype(jnp.bfloat16)
    low = (value - high.astype(jnp.float32)).astype(jnp.bfloat16)
    return high, low


def split_outside(value):
    high = lax.reduce_precision(value, exponent_bits=8, mantissa_bits=7)
    return high.astype(jnp.bfloat16), (value - high).astype(jnp.bfloat16)


def dot3(lhs, rhs_high, rhs_low):
    lhs_high, lhs_low = split_bf16(lhs)
    out = jnp.dot(lhs_high, rhs_high, preferred_element_type=jnp.float32)
    out += jnp.dot(lhs_high, rhs_low, preferred_element_type=jnp.float32)
    out += jnp.dot(lhs_low, rhs_high, preferred_element_type=jnp.float32)
    return out


def depth_kernel(rows_ref, fz_hi, fz_lo, a_ref, b_ref, q_hi, q_lo, wc_ref, ws_ref, out_ref):
    xdev, depth = a_ref.shape
    half = depth // 2
    width = wc_ref.shape[1]
    spec = dot3(rows_ref[...], fz_hi[...], fz_lo[...])
    spec = spec.reshape(-1, xdev, depth)
    scale_a = a_ref[...][None]
    scale_b = b_ref[...][None]
    low, high = spec[..., :half], spec[..., half:]
    out_low = low * scale_a[..., :half] + high * scale_b[..., :half]
    out_high = high * scale_a[..., half:] + low * scale_b[..., half:]
    turned = jnp.concatenate([out_low, out_high], axis=-1).reshape(-1, depth)
    mixed = dot3(turned, q_hi[...], q_lo[...]).reshape(-1, xdev, 2 * width)
    mix_c, mix_s = mixed[..., :width], mixed[..., width:]
    wc = wc_ref[...][None]
    ws = ws_ref[...][None]
    out_ref[:, :width] = jnp.sum(wc * mix_c - ws * mix_s, axis=1)
    out_ref[:, width:] = -jnp.sum(wc * mix_s + ws * mix_c, axis=1)


def depth_stage(rows, fz, scale_a, scale_b, depth_to_line, line_wc, line_ws):
    count, depth = rows.shape
    xdev = scale_a.shape[0]
    width = line_wc.shape[1]
    ydev = count // xdev
    block = YBLOCK * xdev
    fz_hi, fz_lo = split_outside(fz)
    q_hi, q_lo = split_outside(depth_to_line)
    whole = lambda i: (0, 0)
    return pl.pallas_call(
        depth_kernel,
        grid=(ydev // YBLOCK,),
        in_specs=[
            pl.BlockSpec((block, depth), lambda i: (i, 0)),
            pl.BlockSpec((depth, depth), whole),
            pl.BlockSpec((depth, depth), whole),
            pl.BlockSpec((xdev, depth), whole),
            pl.BlockSpec((xdev, depth), whole),
            pl.BlockSpec((depth, 2 * width), whole),
            pl.BlockSpec((depth, 2 * width), whole),
            pl.BlockSpec((xdev, width), whole),
            pl.BlockSpec((xdev, width), whole),
        ],
        out_specs=pl.BlockSpec((YBLOCK, 2 * width), lambda i: (i, 0)),
        out_shape=jax.ShapeDtypeStruct((ydev, 2 * width), jnp.float32),
        interpret=INTERPRET,
    )(rows, fz_hi, fz_lo, scale_a, scale_b, q_hi, q_lo, line_wc, line_ws)


def wave_pair(first, second, length):
    turns = jnp.mod(first[:, None] * second[None, :], length).astype(jnp.float32)
    angle = 2.0 * math.pi / length * turns
    return (jnp.cos(angle), jnp.sin(angle))


def ramp_pair(shifts, length):
    freq = jnp.arange(length, dtype=jnp.int32)
    signed = jnp.mod(freq + length // 2, length) - length // 2
    turns = jnp.mod(shifts[..., None] * signed, SUB * length).astype(jnp.float32)
    angle = 2.0 * math.pi / (SUB * length) * turns
    return (jnp.cos(angle), jnp.sin(angle))


def signed_turns(shifts, freq, length):
    signed = jnp.mod(freq + length // 2, length) - length // 2
    turns = jnp.mod(shifts[..., None] * signed, SUB * length).astype(jnp.float32)
    angle = 2.0 * math.pi / (SUB * length) * turns
    return (jnp.cos(angle), jnp.sin(angle))


def packed_forward(length):
    half = length // 2
    pos = jnp.arange(length, dtype=jnp.int32)
    freq = jnp.arange(half, dtype=jnp.int32)
    wc, ws = wave_pair(pos, freq, length)
    alt = jnp.where(pos % 2 == 0, 1.0, -1.0).astype(jnp.float32)
    im_cols = jnp.concatenate([alt[:, None], -ws[:, 1:]], axis=1)
    return jnp.concatenate([wc, im_cols], axis=1)


def packed_inverse(length):
    half = length // 2
    pos = jnp.arange(length, dtype=jnp.int32)
    freq = jnp.arange(half, dtype=jnp.int32)
    wc, ws = wave_pair(freq, pos, length)
    alt = jnp.where(pos % 2 == 0, 1.0, -1.0).astype(jnp.float32)
    weight = jnp.where(freq == 0, 1.0, 2.0).astype(jnp.float32)[:, None]
    re_rows = wc * weight
    im_rows = jnp.concatenate([alt[None, :], -2.0 * ws[1:]], axis=0)
    return jnp.concatenate([re_rows, im_rows], axis=0) / length


def packed_phase(shifts, length):
    half = length // 2
    freq = jnp.arange(half + 1, dtype=jnp.int32)
    cos_k, sin_k = signed_turns(shifts, freq, length)
    zero = jnp.zeros_like(sin_k[..., :1])
    scale_a = jnp.concatenate([cos_k[..., :half], cos_k[..., half:], cos_k[..., 1:half]], axis=-1)
    scale_b = jnp.concatenate([zero, sin_k[..., 1:half], zero, -sin_k[..., 1:half]], axis=-1)
    return scale_a, scale_b


def turn(spec, scale_a, scale_b):
    half = spec.shape[-1] // 2
    low, high = spec[..., :half], spec[..., half:]
    out_low = low * scale_a[..., :half] + high * scale_b[..., :half]
    out_high = high * scale_a[..., half:] + low * scale_b[..., half:]
    return jnp.concatenate([out_low, out_high], axis=-1)


def on_device(volume, shift_x, shift_z, mask, measured):
    zparts = lax.axis_size("zblock")
    zindex = lax.axis_index("zblock")
    yindex = lax.axis_index("yslab")
    ydev, zdev, width = volume.shape
    depth = zdev * zparts
    xdev = width // zparts
    zstart = zindex * zdev
    xstart = zindex * xdev
    tilts = shift_x.shape[0]
    scale = 1.0 / math.sqrt(depth * width)
    half = width // 2

    fx = packed_forward(width)
    gx = packed_inverse(width)
    fz = packed_forward(depth)
    gz = packed_inverse(depth)

    xfreq = jnp.arange(width, dtype=jnp.int32)
    xlocal = jnp.arange(xdev, dtype=jnp.int32) + xstart
    line_wc, line_ws = wave_pair(xlocal, xfreq, width)

    rows = volume.reshape(ydev * zdev, width)
    spec_x = jnp.matmul(rows, fx, precision=HIGH).reshape(ydev, zdev, width)

    partial = []
    for tilt in range(tilts):
        local_shift = lax.dynamic_slice_in_dim(shift_x[tilt], zstart, zdev, 0)
        near_a, near_b = packed_phase(local_shift, width)
        turned = turn(spec_x, near_a[None], near_b[None])
        first = jnp.matmul(turned.reshape(ydev * zdev, width), gx, precision=HIGH)
        first = first.reshape(ydev, zdev, width)
        columns = lax.all_to_all(first, "zblock", split_axis=2, concat_axis=1, tiled=True)
        columns = jnp.transpose(columns, (0, 2, 1))
        column_shift = lax.dynamic_slice_in_dim(shift_z[tilt], xstart, xdev, 0)
        col_a, col_b = packed_phase(column_shift, depth)
        ph_c, ph_s = ramp_pair(shift_x[tilt], width)
        depth_to_line = jnp.matmul(gz, jnp.concatenate([ph_c, ph_s], axis=1), precision=HIGH)
        mixed = depth_stage(
            columns.reshape(ydev * xdev, depth), fz, col_a, col_b, depth_to_line, line_wc, line_ws
        )
        full_re, full_im = mixed[:, :width], mixed[:, width:]
        partial.append(jnp.stack((full_re, full_im)) * scale)

    pieces = jnp.stack(partial)
    kdev = width // zparts
    pieces = pieces.reshape(tilts, 2, ydev, zparts, kdev)
    pieces = jnp.moveaxis(pieces, 3, 0)
    pieces = lax.all_to_all(pieces, "zblock", 0, 0, tiled=True)
    lines = jnp.sum(pieces, axis=0)
    spec_re = lines[:, 0]
    spec_im = lines[:, 1]
    yparts = lax.axis_size("yslab")
    rows_all = ydev * yparts
    ylocal = jnp.arange(ydev, dtype=jnp.int32) + yindex * ydev
    kfreq = jnp.arange(rows_all, dtype=jnp.int32)
    wave_cos, wave_sin = wave_pair(kfreq, ylocal, rows_all)
    term_re = jnp.einsum("ky,tyx->ktx", wave_cos, spec_re, precision=HIGH) + jnp.einsum(
        "ky,tyx->ktx", wave_sin, spec_im, precision=HIGH
    )
    term_im = jnp.einsum("ky,tyx->ktx", wave_cos, spec_im, precision=HIGH) - jnp.einsum(
        "ky,tyx->ktx", wave_sin, spec_re, precision=HIGH
    )
    terms = jnp.stack((term_re, term_im), axis=1) / math.sqrt(rows_all)
    terms = terms.reshape((yparts, ydev) + terms.shape[1:])
    terms = lax.all_to_all(terms, "yslab", 0, 0, tiled=True)
    gathered = jnp.sum(terms, axis=0)
    spectrum = jnp.transpose(gathered, (1, 2, 0, 3))
    weight = mask.astype(jnp.float32)[None]
    return spectrum + weight * (measured - spectrum)


def solution(mesh):
    in_specs = (
        P("yslab", "zblock", None),
        P(),
        P(),
        P(None, "yslab", "zblock"),
        P(None, None, "yslab", "zblock"),
    )
    out_specs = P(None, None, "yslab", "zblock")
    return jax.shard_map(
        on_device, mesh=mesh, in_specs=in_specs, out_specs=out_specs, check_vma=False
    )
```

```python
import math
import os

import jax
import jax.numpy as jnp
from jax import lax
from jax.experimental import pallas as pl
from jax.sharding import PartitionSpec as P

SUB = 64


HIGH = lax.Precision.HIGH
INTERPRET = os.environ.get("SOL_INTERPRET") == "1"
YBLOCK = 32


def split_bf16(value):
    high = value.astype(jnp.bfloat16)
    low = (value - high.astype(jnp.float32)).astype(jnp.bfloat16)
    return high, low


def split_outside(value):
    high = lax.reduce_precision(value, exponent_bits=8, mantissa_bits=7)
    return high.astype(jnp.bfloat16), (value - high).astype(jnp.bfloat16)


def dot3(lhs, rhs_high, rhs_low):
    lhs_high, lhs_low = split_bf16(lhs)
    out = jnp.dot(lhs_high, rhs_high, preferred_element_type=jnp.float32)
    out += jnp.dot(lhs_high, rhs_low, preferred_element_type=jnp.float32)
    out += jnp.dot(lhs_low, rhs_high, preferred_element_type=jnp.float32)
    return out


def depth_kernel(rows_ref, fz_hi, fz_lo, a_ref, b_ref, q_hi, q_lo, wc_ref, ws_ref, out_ref):
    xdev, depth = a_ref.shape
    half = depth // 2
    width = wc_ref.shape[1]
    spec = dot3(rows_ref[...], fz_hi[...], fz_lo[...])
    spec = spec.reshape(-1, xdev, depth)
    scale_a = a_ref[...][None]
    scale_b = b_ref[...][None]
    low, high = spec[..., :half], spec[..., half:]
    out_low = low * scale_a[..., :half] + high * scale_b[..., :half]
    out_high = high * scale_a[..., half:] + low * scale_b[..., half:]
    turned = jnp.concatenate([out_low, out_high], axis=-1).reshape(-1, depth)
    mixed = dot3(turned, q_hi[...], q_lo[...]).reshape(-1, xdev, 2 * width)
    mix_c, mix_s = mixed[..., :width], mixed[..., width:]
    wc = wc_ref[...][None]
    ws = ws_ref[...][None]
    out_ref[:, :width] = jnp.sum(wc * mix_c - ws * mix_s, axis=1)
    out_ref[:, width:] = -jnp.sum(wc * mix_s + ws * mix_c, axis=1)


def depth_stage(rows, fz, scale_a, scale_b, depth_to_line, line_wc, line_ws):
    count, depth = rows.shape
    xdev = scale_a.shape[0]
    width = line_wc.shape[1]
    ydev = count // xdev
    block = YBLOCK * xdev
    fz_hi, fz_lo = split_outside(fz)
    q_hi, q_lo = split_outside(depth_to_line)
    whole = lambda i: (0, 0)
    return pl.pallas_call(
        depth_kernel,
        grid=(ydev // YBLOCK,),
        in_specs=[
            pl.BlockSpec((block, depth), lambda i: (i, 0)),
            pl.BlockSpec((depth, depth), whole),
            pl.BlockSpec((depth, depth), whole),
            pl.BlockSpec((xdev, depth), whole),
            pl.BlockSpec((xdev, depth), whole),
            pl.BlockSpec((depth, 2 * width), whole),
            pl.BlockSpec((depth, 2 * width), whole),
            pl.BlockSpec((xdev, width), whole),
            pl.BlockSpec((xdev, width), whole),
        ],
        out_specs=pl.BlockSpec((YBLOCK, 2 * width), lambda i: (i, 0)),
        out_shape=jax.ShapeDtypeStruct((ydev, 2 * width), jnp.float32),
        interpret=INTERPRET,
    )(rows, fz_hi, fz_lo, scale_a, scale_b, q_hi, q_lo, line_wc, line_ws)


def wave_pair(first, second, length):
    turns = jnp.mod(first[:, None] * second[None, :], length).astype(jnp.float32)
    angle = 2.0 * math.pi / length * turns
    return (jnp.cos(angle), jnp.sin(angle))


def ramp_pair(shifts, length):
    freq = jnp.arange(length, dtype=jnp.int32)
    signed = jnp.mod(freq + length // 2, length) - length // 2
    turns = jnp.mod(shifts[..., None] * signed, SUB * length).astype(jnp.float32)
    angle = 2.0 * math.pi / (SUB * length) * turns
    return (jnp.cos(angle), jnp.sin(angle))


def signed_turns(shifts, freq, length):
    signed = jnp.mod(freq + length // 2, length) - length // 2
    turns = jnp.mod(shifts[..., None] * signed, SUB * length).astype(jnp.float32)
    angle = 2.0 * math.pi / (SUB * length) * turns
    return (jnp.cos(angle), jnp.sin(angle))


def packed_forward(length):
    half = length // 2
    pos = jnp.arange(length, dtype=jnp.int32)
    freq = jnp.arange(half, dtype=jnp.int32)
    wc, ws = wave_pair(pos, freq, length)
    alt = jnp.where(pos % 2 == 0, 1.0, -1.0).astype(jnp.float32)
    im_cols = jnp.concatenate([alt[:, None], -ws[:, 1:]], axis=1)
    return jnp.concatenate([wc, im_cols], axis=1)


def packed_inverse(length):
    half = length // 2
    pos = jnp.arange(length, dtype=jnp.int32)
    freq = jnp.arange(half, dtype=jnp.int32)
    wc, ws = wave_pair(freq, pos, length)
    alt = jnp.where(pos % 2 == 0, 1.0, -1.0).astype(jnp.float32)
    weight = jnp.where(freq == 0, 1.0, 2.0).astype(jnp.float32)[:, None]
    re_rows = wc * weight
    im_rows = jnp.concatenate([alt[None, :], -2.0 * ws[1:]], axis=0)
    return jnp.concatenate([re_rows, im_rows], axis=0) / length


def packed_phase(shifts, length):
    half = length // 2
    freq = jnp.arange(half + 1, dtype=jnp.int32)
    cos_k, sin_k = signed_turns(shifts, freq, length)
    zero = jnp.zeros_like(sin_k[..., :1])
    scale_a = jnp.concatenate([cos_k[..., :half], cos_k[..., half:], cos_k[..., 1:half]], axis=-1)
    scale_b = jnp.concatenate([zero, sin_k[..., 1:half], zero, -sin_k[..., 1:half]], axis=-1)
    return scale_a, scale_b


def turn(spec, scale_a, scale_b):
    half = spec.shape[-1] // 2
    low, high = spec[..., :half], spec[..., half:]
    out_low = low * scale_a[..., :half] + high * scale_b[..., :half]
    out_high = high * scale_a[..., half:] + low * scale_b[..., half:]
    return jnp.concatenate([out_low, out_high], axis=-1)


def on_device(volume, shift_x, shift_z, mask, measured):
    zparts = lax.axis_size("zblock")
    zindex = lax.axis_index("zblock")
    yindex = lax.axis_index("yslab")
    ydev, zdev, width = volume.shape
    depth = zdev * zparts
    xdev = width // zparts
    zstart = zindex * zdev
    xstart = zindex * xdev
    tilts = shift_x.shape[0]
    scale = 1.0 / math.sqrt(depth * width)
    half = width // 2

    fx = packed_forward(width)
    gx = packed_inverse(width)
    fz = packed_forward(depth)
    gz = packed_inverse(depth)

    xfreq = jnp.arange(width, dtype=jnp.int32)
    xlocal = jnp.arange(xdev, dtype=jnp.int32) + xstart
    line_wc, line_ws = wave_pair(xlocal, xfreq, width)

    rows = volume.reshape(ydev * zdev, width)
    spec_x = jnp.matmul(rows, fx, precision=HIGH).reshape(ydev, zdev, width)

    partial = []
    for tilt in range(tilts):
        local_shift = lax.dynamic_slice_in_dim(shift_x[tilt], zstart, zdev, 0)
        near_a, near_b = packed_phase(local_shift, width)
        turned = turn(spec_x, near_a[None], near_b[None])
        first = jnp.matmul(turned.reshape(ydev * zdev, width), gx, precision=HIGH)
        first = first.reshape(ydev, zdev, width)
        columns = lax.all_to_all(first, "zblock", split_axis=2, concat_axis=1, tiled=True)
        columns = jnp.transpose(columns, (0, 2, 1))
        column_shift = lax.dynamic_slice_in_dim(shift_z[tilt], xstart, xdev, 0)
        col_a, col_b = packed_phase(column_shift, depth)
        ph_c, ph_s = ramp_pair(shift_x[tilt], width)
        depth_to_line = jnp.matmul(gz, jnp.concatenate([ph_c, ph_s], axis=1), precision=HIGH)
        mixed = depth_stage(
            columns.reshape(ydev * xdev, depth), fz, col_a, col_b, depth_to_line, line_wc, line_ws
        )
        full_re, full_im = mixed[:, :width], mixed[:, width:]
        piece = jnp.stack((full_re, full_im)) * scale
        piece = jnp.moveaxis(piece.reshape(2, ydev, zparts, width // zparts), 2, 0)
        piece = lax.all_to_all(piece, "zblock", 0, 0, tiled=True)
        partial.append(jnp.sum(piece, axis=0))

    lines = jnp.stack(partial)
    spec_re = lines[:, 0]
    spec_im = lines[:, 1]
    yparts = lax.axis_size("yslab")
    rows_all = ydev * yparts
    ylocal = jnp.arange(ydev, dtype=jnp.int32) + yindex * ydev
    kfreq = jnp.arange(rows_all, dtype=jnp.int32)
    wave_cos, wave_sin = wave_pair(kfreq, ylocal, rows_all)
    term_re = jnp.einsum("ky,tyx->ktx", wave_cos, spec_re, precision=HIGH) + jnp.einsum(
        "ky,tyx->ktx", wave_sin, spec_im, precision=HIGH
    )
    term_im = jnp.einsum("ky,tyx->ktx", wave_cos, spec_im, precision=HIGH) - jnp.einsum(
        "ky,tyx->ktx", wave_sin, spec_re, precision=HIGH
    )
    terms = jnp.stack((term_re, term_im), axis=1) / math.sqrt(rows_all)
    terms = terms.reshape((yparts, ydev) + terms.shape[1:])
    terms = lax.all_to_all(terms, "yslab", 0, 0, tiled=True)
    gathered = jnp.sum(terms, axis=0)
    spectrum = jnp.transpose(gathered, (1, 2, 0, 3))
    weight = mask.astype(jnp.float32)[None]
    return spectrum + weight * (measured - spectrum)


def solution(mesh):
    in_specs = (
        P("yslab", "zblock", None),
        P(),
        P(),
        P(None, "yslab", "zblock"),
        P(None, None, "yslab", "zblock"),
    )
    out_specs = P(None, None, "yslab", "zblock")
    return jax.shard_map(
        on_device, mesh=mesh, in_specs=in_specs, out_specs=out_specs, check_vma=False
    )
```

```python
import math
import os

import jax
import jax.numpy as jnp
from jax import lax
from jax.experimental import pallas as pl
from jax.sharding import PartitionSpec as P

SUB = 64


HIGH = lax.Precision.HIGH
INTERPRET = os.environ.get("SOL_INTERPRET") == "1"
YBLOCK = 32


def split_bf16(value):
    high = value.astype(jnp.bfloat16)
    low = (value - high.astype(jnp.float32)).astype(jnp.bfloat16)
    return high, low


def split_outside(value):
    high = lax.reduce_precision(value, exponent_bits=8, mantissa_bits=7)
    return high.astype(jnp.bfloat16), (value - high).astype(jnp.bfloat16)


def dot3(lhs, rhs_high, rhs_low):
    lhs_high, lhs_low = split_bf16(lhs)
    out = jnp.dot(lhs_high, rhs_high, preferred_element_type=jnp.float32)
    out += jnp.dot(lhs_high, rhs_low, preferred_element_type=jnp.float32)
    out += jnp.dot(lhs_low, rhs_high, preferred_element_type=jnp.float32)
    return out


def depth_kernel(rows_ref, fz_hi, fz_lo, a_ref, b_ref, q_hi, q_lo, wc_ref, ws_ref, out_ref):
    xdev, depth = a_ref.shape
    half = depth // 2
    width = wc_ref.shape[1]
    spec = dot3(rows_ref[...], fz_hi[...], fz_lo[...])
    spec = spec.reshape(-1, xdev, depth)
    scale_a = a_ref[...][None]
    scale_b = b_ref[...][None]
    low, high = spec[..., :half], spec[..., half:]
    out_low = low * scale_a[..., :half] + high * scale_b[..., :half]
    out_high = high * scale_a[..., half:] + low * scale_b[..., half:]
    turned = jnp.concatenate([out_low, out_high], axis=-1).reshape(-1, depth)
    mixed = dot3(turned, q_hi[...], q_lo[...]).reshape(-1, xdev, 2 * width)
    mix_c, mix_s = mixed[..., :width], mixed[..., width:]
    wc = wc_ref[...][None]
    ws = ws_ref[...][None]
    out_ref[:, :width] = jnp.sum(wc * mix_c - ws * mix_s, axis=1)
    out_ref[:, width:] = -jnp.sum(wc * mix_s + ws * mix_c, axis=1)


def depth_stage(rows, fz, scale_a, scale_b, depth_to_line, line_wc, line_ws):
    count, depth = rows.shape
    xdev = scale_a.shape[0]
    width = line_wc.shape[1]
    ydev = count // xdev
    block = YBLOCK * xdev
    fz_hi, fz_lo = split_outside(fz)
    q_hi, q_lo = split_outside(depth_to_line)
    whole = lambda i: (0, 0)
    return pl.pallas_call(
        depth_kernel,
        grid=(ydev // YBLOCK,),
        in_specs=[
            pl.BlockSpec((block, depth), lambda i: (i, 0)),
            pl.BlockSpec((depth, depth), whole),
            pl.BlockSpec((depth, depth), whole),
            pl.BlockSpec((xdev, depth), whole),
            pl.BlockSpec((xdev, depth), whole),
            pl.BlockSpec((depth, 2 * width), whole),
            pl.BlockSpec((depth, 2 * width), whole),
            pl.BlockSpec((xdev, width), whole),
            pl.BlockSpec((xdev, width), whole),
        ],
        out_specs=pl.BlockSpec((YBLOCK, 2 * width), lambda i: (i, 0)),
        out_shape=jax.ShapeDtypeStruct((ydev, 2 * width), jnp.float32),
        interpret=INTERPRET,
    )(rows, fz_hi, fz_lo, scale_a, scale_b, q_hi, q_lo, line_wc, line_ws)


def wave_pair(first, second, length):
    turns = jnp.mod(first[:, None] * second[None, :], length).astype(jnp.float32)
    angle = 2.0 * math.pi / length * turns
    return (jnp.cos(angle), jnp.sin(angle))


def ramp_pair(shifts, length):
    freq = jnp.arange(length, dtype=jnp.int32)
    signed = jnp.mod(freq + length // 2, length) - length // 2
    turns = jnp.mod(shifts[..., None] * signed, SUB * length).astype(jnp.float32)
    angle = 2.0 * math.pi / (SUB * length) * turns
    return (jnp.cos(angle), jnp.sin(angle))


def signed_turns(shifts, freq, length):
    signed = jnp.mod(freq + length // 2, length) - length // 2
    turns = jnp.mod(shifts[..., None] * signed, SUB * length).astype(jnp.float32)
    angle = 2.0 * math.pi / (SUB * length) * turns
    return (jnp.cos(angle), jnp.sin(angle))


def packed_forward(length):
    half = length // 2
    pos = jnp.arange(length, dtype=jnp.int32)
    freq = jnp.arange(half, dtype=jnp.int32)
    wc, ws = wave_pair(pos, freq, length)
    alt = jnp.where(pos % 2 == 0, 1.0, -1.0).astype(jnp.float32)
    im_cols = jnp.concatenate([alt[:, None], -ws[:, 1:]], axis=1)
    return jnp.concatenate([wc, im_cols], axis=1)


def packed_inverse(length):
    half = length // 2
    pos = jnp.arange(length, dtype=jnp.int32)
    freq = jnp.arange(half, dtype=jnp.int32)
    wc, ws = wave_pair(freq, pos, length)
    alt = jnp.where(pos % 2 == 0, 1.0, -1.0).astype(jnp.float32)
    weight = jnp.where(freq == 0, 1.0, 2.0).astype(jnp.float32)[:, None]
    re_rows = wc * weight
    im_rows = jnp.concatenate([alt[None, :], -2.0 * ws[1:]], axis=0)
    return jnp.concatenate([re_rows, im_rows], axis=0) / length


def packed_phase(shifts, length):
    half = length // 2
    freq = jnp.arange(half + 1, dtype=jnp.int32)
    cos_k, sin_k = signed_turns(shifts, freq, length)
    zero = jnp.zeros_like(sin_k[..., :1])
    scale_a = jnp.concatenate([cos_k[..., :half], cos_k[..., half:], cos_k[..., 1:half]], axis=-1)
    scale_b = jnp.concatenate([zero, sin_k[..., 1:half], zero, -sin_k[..., 1:half]], axis=-1)
    return scale_a, scale_b


def turn(spec, scale_a, scale_b):
    half = spec.shape[-1] // 2
    low, high = spec[..., :half], spec[..., half:]
    out_low = low * scale_a[..., :half] + high * scale_b[..., :half]
    out_high = high * scale_a[..., half:] + low * scale_b[..., half:]
    return jnp.concatenate([out_low, out_high], axis=-1)


def on_device(volume, shift_x, shift_z, mask, measured):
    zparts = lax.axis_size("zblock")
    zindex = lax.axis_index("zblock")
    yindex = lax.axis_index("yslab")
    ydev, zdev, width = volume.shape
    depth = zdev * zparts
    xdev = width // zparts
    zstart = zindex * zdev
    xstart = zindex * xdev
    tilts = shift_x.shape[0]
    scale = 1.0 / math.sqrt(depth * width)
    half = width // 2

    fx = packed_forward(width)
    gx = packed_inverse(width)
    fz = packed_forward(depth)
    gz = packed_inverse(depth)

    xfreq = jnp.arange(width, dtype=jnp.int32)
    xlocal = jnp.arange(xdev, dtype=jnp.int32) + xstart
    line_wc, line_ws = wave_pair(xlocal, xfreq, width)

    rows = volume.reshape(ydev * zdev, width)
    spec_x = jnp.matmul(rows, fx, precision=HIGH).reshape(ydev, zdev, width)

    partial = []
    for tilt in range(tilts):
        local_shift = lax.dynamic_slice_in_dim(shift_x[tilt], zstart, zdev, 0)
        near_a, near_b = packed_phase(local_shift, width)
        turned = turn(spec_x, near_a[None], near_b[None])
        first = jnp.matmul(turned.reshape(ydev * zdev, width), gx, precision=HIGH)
        first = first.reshape(ydev, zdev, width)
        send = first.reshape(ydev, zdev, zparts, xdev).transpose(2, 3, 1, 0)
        landed = lax.all_to_all(send, "zblock", 0, 0, tiled=True)
        columns = landed.transpose(3, 1, 0, 2)
        column_shift = lax.dynamic_slice_in_dim(shift_z[tilt], xstart, xdev, 0)
        col_a, col_b = packed_phase(column_shift, depth)
        ph_c, ph_s = ramp_pair(shift_x[tilt], width)
        depth_to_line = jnp.matmul(gz, jnp.concatenate([ph_c, ph_s], axis=1), precision=HIGH)
        mixed = depth_stage(
            columns.reshape(ydev * xdev, depth), fz, col_a, col_b, depth_to_line, line_wc, line_ws
        )
        full_re, full_im = mixed[:, :width], mixed[:, width:]
        partial.append(jnp.stack((full_re, full_im)) * scale)

    pieces = jnp.stack(partial)
    kdev = width // zparts
    pieces = pieces.reshape(tilts, 2, ydev, zparts, kdev)
    pieces = jnp.moveaxis(pieces, 3, 0)
    pieces = lax.all_to_all(pieces, "zblock", 0, 0, tiled=True)
    lines = jnp.sum(pieces, axis=0)
    spec_re = lines[:, 0]
    spec_im = lines[:, 1]
    yparts = lax.axis_size("yslab")
    rows_all = ydev * yparts
    ylocal = jnp.arange(ydev, dtype=jnp.int32) + yindex * ydev
    kfreq = jnp.arange(rows_all, dtype=jnp.int32)
    wave_cos, wave_sin = wave_pair(kfreq, ylocal, rows_all)
    term_re = jnp.einsum("ky,tyx->ktx", wave_cos, spec_re, precision=HIGH) + jnp.einsum(
        "ky,tyx->ktx", wave_sin, spec_im, precision=HIGH
    )
    term_im = jnp.einsum("ky,tyx->ktx", wave_cos, spec_im, precision=HIGH) - jnp.einsum(
        "ky,tyx->ktx", wave_sin, spec_re, precision=HIGH
    )
    terms = jnp.stack((term_re, term_im), axis=1) / math.sqrt(rows_all)
    terms = terms.reshape((yparts, ydev) + terms.shape[1:])
    terms = lax.all_to_all(terms, "yslab", 0, 0, tiled=True)
    gathered = jnp.sum(terms, axis=0)
    spectrum = jnp.transpose(gathered, (1, 2, 0, 3))
    weight = mask.astype(jnp.float32)[None]
    return spectrum + weight * (measured - spectrum)


def solution(mesh):
    in_specs = (
        P("yslab", "zblock", None),
        P(),
        P(),
        P(None, "yslab", "zblock"),
        P(None, None, "yslab", "zblock"),
    )
    out_specs = P(None, None, "yslab", "zblock")
    return jax.shard_map(
        on_device, mesh=mesh, in_specs=in_specs, out_specs=out_specs, check_vma=False
    )
```

```python
import math
import os

import jax
import jax.numpy as jnp
from jax import lax
from jax.experimental import pallas as pl
from jax.sharding import PartitionSpec as P

SUB = 64


HIGH = lax.Precision.HIGH
INTERPRET = os.environ.get("SOL_INTERPRET") == "1"
YBLOCK = 32


def split_bf16(value):
    high = value.astype(jnp.bfloat16)
    low = (value - high.astype(jnp.float32)).astype(jnp.bfloat16)
    return high, low


def split_outside(value):
    high = lax.reduce_precision(value, exponent_bits=8, mantissa_bits=7)
    return high.astype(jnp.bfloat16), (value - high).astype(jnp.bfloat16)


def dot3(lhs, rhs_high, rhs_low):
    lhs_high, lhs_low = split_bf16(lhs)
    out = jnp.dot(lhs_high, rhs_high, preferred_element_type=jnp.float32)
    out += jnp.dot(lhs_high, rhs_low, preferred_element_type=jnp.float32)
    out += jnp.dot(lhs_low, rhs_high, preferred_element_type=jnp.float32)
    return out


def depth_kernel(rows_ref, fz_hi, fz_lo, a_ref, b_ref, q_hi, q_lo, wc_ref, ws_ref, out_ref):
    xdev, depth = a_ref.shape
    half = depth // 2
    width = wc_ref.shape[1]
    spec = dot3(rows_ref[...], fz_hi[...], fz_lo[...])
    spec = spec.reshape(-1, xdev, depth)
    scale_a = a_ref[...][None]
    scale_b = b_ref[...][None]
    low, high = spec[..., :half], spec[..., half:]
    out_low = low * scale_a[..., :half] + high * scale_b[..., :half]
    out_high = high * scale_a[..., half:] + low * scale_b[..., half:]
    turned = jnp.concatenate([out_low, out_high], axis=-1).reshape(-1, depth)
    mixed = dot3(turned, q_hi[...], q_lo[...]).reshape(-1, xdev, 2 * width)
    mix_c, mix_s = mixed[..., :width], mixed[..., width:]
    wc = wc_ref[...][None]
    ws = ws_ref[...][None]
    out_ref[:, :width] = jnp.sum(wc * mix_c - ws * mix_s, axis=1)
    out_ref[:, width:] = -jnp.sum(wc * mix_s + ws * mix_c, axis=1)


def forward_kernel(rows_ref, f_hi, f_lo, out_ref):
    out_ref[...] = dot3(rows_ref[...], f_hi[...], f_lo[...])


def forward_stage(rows, matrix):
    count, width = rows.shape
    block = 256
    f_hi, f_lo = split_outside(matrix)
    whole = lambda i: (0, 0)
    return pl.pallas_call(
        forward_kernel,
        grid=(count // block,),
        in_specs=[
            pl.BlockSpec((block, width), lambda i: (i, 0)),
            pl.BlockSpec((width, width), whole),
            pl.BlockSpec((width, width), whole),
        ],
        out_specs=pl.BlockSpec((block, width), lambda i: (i, 0)),
        out_shape=jax.ShapeDtypeStruct((count, width), jnp.float32),
        interpret=INTERPRET,
    )(rows, f_hi, f_lo)


def depth_stage(rows, fz, scale_a, scale_b, depth_to_line, line_wc, line_ws):
    count, depth = rows.shape
    xdev = scale_a.shape[0]
    width = line_wc.shape[1]
    ydev = count // xdev
    block = YBLOCK * xdev
    fz_hi, fz_lo = split_outside(fz)
    q_hi, q_lo = split_outside(depth_to_line)
    whole = lambda i: (0, 0)
    return pl.pallas_call(
        depth_kernel,
        grid=(ydev // YBLOCK,),
        in_specs=[
            pl.BlockSpec((block, depth), lambda i: (i, 0)),
            pl.BlockSpec((depth, depth), whole),
            pl.BlockSpec((depth, depth), whole),
            pl.BlockSpec((xdev, depth), whole),
            pl.BlockSpec((xdev, depth), whole),
            pl.BlockSpec((depth, 2 * width), whole),
            pl.BlockSpec((depth, 2 * width), whole),
            pl.BlockSpec((xdev, width), whole),
            pl.BlockSpec((xdev, width), whole),
        ],
        out_specs=pl.BlockSpec((YBLOCK, 2 * width), lambda i: (i, 0)),
        out_shape=jax.ShapeDtypeStruct((ydev, 2 * width), jnp.float32),
        interpret=INTERPRET,
    )(rows, fz_hi, fz_lo, scale_a, scale_b, q_hi, q_lo, line_wc, line_ws)


def wave_pair(first, second, length):
    turns = jnp.mod(first[:, None] * second[None, :], length).astype(jnp.float32)
    angle = 2.0 * math.pi / length * turns
    return (jnp.cos(angle), jnp.sin(angle))


def ramp_pair(shifts, length):
    freq = jnp.arange(length, dtype=jnp.int32)
    signed = jnp.mod(freq + length // 2, length) - length // 2
    turns = jnp.mod(shifts[..., None] * signed, SUB * length).astype(jnp.float32)
    angle = 2.0 * math.pi / (SUB * length) * turns
    return (jnp.cos(angle), jnp.sin(angle))


def signed_turns(shifts, freq, length):
    signed = jnp.mod(freq + length // 2, length) - length // 2
    turns = jnp.mod(shifts[..., None] * signed, SUB * length).astype(jnp.float32)
    angle = 2.0 * math.pi / (SUB * length) * turns
    return (jnp.cos(angle), jnp.sin(angle))


def packed_forward(length):
    half = length // 2
    pos = jnp.arange(length, dtype=jnp.int32)
    freq = jnp.arange(half, dtype=jnp.int32)
    wc, ws = wave_pair(pos, freq, length)
    alt = jnp.where(pos % 2 == 0, 1.0, -1.0).astype(jnp.float32)
    im_cols = jnp.concatenate([alt[:, None], -ws[:, 1:]], axis=1)
    return jnp.concatenate([wc, im_cols], axis=1)


def packed_inverse(length):
    half = length // 2
    pos = jnp.arange(length, dtype=jnp.int32)
    freq = jnp.arange(half, dtype=jnp.int32)
    wc, ws = wave_pair(freq, pos, length)
    alt = jnp.where(pos % 2 == 0, 1.0, -1.0).astype(jnp.float32)
    weight = jnp.where(freq == 0, 1.0, 2.0).astype(jnp.float32)[:, None]
    re_rows = wc * weight
    im_rows = jnp.concatenate([alt[None, :], -2.0 * ws[1:]], axis=0)
    return jnp.concatenate([re_rows, im_rows], axis=0) / length


def packed_phase(shifts, length):
    half = length // 2
    freq = jnp.arange(half + 1, dtype=jnp.int32)
    cos_k, sin_k = signed_turns(shifts, freq, length)
    zero = jnp.zeros_like(sin_k[..., :1])
    scale_a = jnp.concatenate([cos_k[..., :half], cos_k[..., half:], cos_k[..., 1:half]], axis=-1)
    scale_b = jnp.concatenate([zero, sin_k[..., 1:half], zero, -sin_k[..., 1:half]], axis=-1)
    return scale_a, scale_b


def turn(spec, scale_a, scale_b):
    half = spec.shape[-1] // 2
    low, high = spec[..., :half], spec[..., half:]
    out_low = low * scale_a[..., :half] + high * scale_b[..., :half]
    out_high = high * scale_a[..., half:] + low * scale_b[..., half:]
    return jnp.concatenate([out_low, out_high], axis=-1)


def on_device(volume, shift_x, shift_z, mask, measured):
    zparts = lax.axis_size("zblock")
    zindex = lax.axis_index("zblock")
    yindex = lax.axis_index("yslab")
    ydev, zdev, width = volume.shape
    depth = zdev * zparts
    xdev = width // zparts
    zstart = zindex * zdev
    xstart = zindex * xdev
    tilts = shift_x.shape[0]
    scale = 1.0 / math.sqrt(depth * width)
    half = width // 2

    fx = packed_forward(width)
    gx = packed_inverse(width)
    fz = packed_forward(depth)
    gz = packed_inverse(depth)

    xfreq = jnp.arange(width, dtype=jnp.int32)
    xlocal = jnp.arange(xdev, dtype=jnp.int32) + xstart
    line_wc, line_ws = wave_pair(xlocal, xfreq, width)

    rows = volume.reshape(ydev * zdev, width)
    spec_x = forward_stage(rows, fx).reshape(ydev, zdev, width)

    partial = []
    for tilt in range(tilts):
        local_shift = lax.dynamic_slice_in_dim(shift_x[tilt], zstart, zdev, 0)
        near_a, near_b = packed_phase(local_shift, width)
        turned = turn(spec_x, near_a[None], near_b[None])
        first = jnp.matmul(turned.reshape(ydev * zdev, width), gx, precision=HIGH)
        first = first.reshape(ydev, zdev, width)
        columns = lax.all_to_all(first, "zblock", split_axis=2, concat_axis=1, tiled=True)
        columns = jnp.transpose(columns, (0, 2, 1))
        column_shift = lax.dynamic_slice_in_dim(shift_z[tilt], xstart, xdev, 0)
        col_a, col_b = packed_phase(column_shift, depth)
        ph_c, ph_s = ramp_pair(shift_x[tilt], width)
        depth_to_line = jnp.matmul(gz, jnp.concatenate([ph_c, ph_s], axis=1), precision=HIGH)
        mixed = depth_stage(
            columns.reshape(ydev * xdev, depth), fz, col_a, col_b, depth_to_line, line_wc, line_ws
        )
        full_re, full_im = mixed[:, :width], mixed[:, width:]
        partial.append(jnp.stack((full_re, full_im)) * scale)

    pieces = jnp.stack(partial)
    kdev = width // zparts
    pieces = pieces.reshape(tilts, 2, ydev, zparts, kdev)
    pieces = jnp.moveaxis(pieces, 3, 0)
    pieces = lax.all_to_all(pieces, "zblock", 0, 0, tiled=True)
    lines = jnp.sum(pieces, axis=0)
    spec_re = lines[:, 0]
    spec_im = lines[:, 1]
    yparts = lax.axis_size("yslab")
    rows_all = ydev * yparts
    ylocal = jnp.arange(ydev, dtype=jnp.int32) + yindex * ydev
    kfreq = jnp.arange(rows_all, dtype=jnp.int32)
    wave_cos, wave_sin = wave_pair(kfreq, ylocal, rows_all)
    term_re = jnp.einsum("ky,tyx->ktx", wave_cos, spec_re, precision=HIGH) + jnp.einsum(
        "ky,tyx->ktx", wave_sin, spec_im, precision=HIGH
    )
    term_im = jnp.einsum("ky,tyx->ktx", wave_cos, spec_im, precision=HIGH) - jnp.einsum(
        "ky,tyx->ktx", wave_sin, spec_re, precision=HIGH
    )
    terms = jnp.stack((term_re, term_im), axis=1) / math.sqrt(rows_all)
    terms = terms.reshape((yparts, ydev) + terms.shape[1:])
    terms = lax.all_to_all(terms, "yslab", 0, 0, tiled=True)
    gathered = jnp.sum(terms, axis=0)
    spectrum = jnp.transpose(gathered, (1, 2, 0, 3))
    weight = mask.astype(jnp.float32)[None]
    return spectrum + weight * (measured - spectrum)


def solution(mesh):
    in_specs = (
        P("yslab", "zblock", None),
        P(),
        P(),
        P(None, "yslab", "zblock"),
        P(None, None, "yslab", "zblock"),
    )
    out_specs = P(None, None, "yslab", "zblock")
    return jax.shard_map(
        on_device, mesh=mesh, in_specs=in_specs, out_specs=out_specs, check_vma=False
    )
```

```python
import math
import os

import jax
import jax.numpy as jnp
from jax import lax
from jax.experimental import pallas as pl
from jax.sharding import PartitionSpec as P

SUB = 64


HIGH = lax.Precision.HIGH
INTERPRET = os.environ.get("SOL_INTERPRET") == "1"
YBLOCK = 32


def split_bf16(value):
    high = value.astype(jnp.bfloat16)
    low = (value - high.astype(jnp.float32)).astype(jnp.bfloat16)
    return high, low


def split_outside(value):
    high = lax.reduce_precision(value, exponent_bits=8, mantissa_bits=7)
    return high.astype(jnp.bfloat16), (value - high).astype(jnp.bfloat16)


def dot3(lhs, rhs_high, rhs_low):
    lhs_high, lhs_low = split_bf16(lhs)
    out = jnp.dot(lhs_high, rhs_high, preferred_element_type=jnp.float32)
    out += jnp.dot(lhs_high, rhs_low, preferred_element_type=jnp.float32)
    out += jnp.dot(lhs_low, rhs_high, preferred_element_type=jnp.float32)
    return out


def depth_kernel(rows_ref, fz_hi, fz_lo, a_ref, b_ref, q_hi, q_lo, wc_ref, ws_ref, out_ref):
    xdev, depth = a_ref.shape
    half = depth // 2
    width = wc_ref.shape[1]
    spec = dot3(rows_ref[...], fz_hi[...], fz_lo[...])
    spec = spec.reshape(-1, xdev, depth)
    scale_a = a_ref[...][None]
    scale_b = b_ref[...][None]
    low, high = spec[..., :half], spec[..., half:]
    out_low = low * scale_a[..., :half] + high * scale_b[..., :half]
    out_high = high * scale_a[..., half:] + low * scale_b[..., half:]
    turned = jnp.concatenate([out_low, out_high], axis=-1).reshape(-1, depth)
    mixed = dot3(turned, q_hi[...], q_lo[...]).reshape(-1, xdev, 2 * width)
    mix_c, mix_s = mixed[..., :width], mixed[..., width:]
    wc = wc_ref[...][None]
    ws = ws_ref[...][None]
    out_ref[:, :width] = jnp.sum(wc * mix_c - ws * mix_s, axis=1)
    out_ref[:, width:] = -jnp.sum(wc * mix_s + ws * mix_c, axis=1)


def forward_kernel(rows_ref, f_hi, f_lo, out_ref):
    out_ref[...] = dot3(rows_ref[...], f_hi[...], f_lo[...])


def forward_stage(rows, matrix):
    count, width = rows.shape
    block = 256
    f_hi, f_lo = split_outside(matrix)
    whole = lambda i: (0, 0)
    return pl.pallas_call(
        forward_kernel,
        grid=(count // block,),
        in_specs=[
            pl.BlockSpec((block, width), lambda i: (i, 0)),
            pl.BlockSpec((width, width), whole),
            pl.BlockSpec((width, width), whole),
        ],
        out_specs=pl.BlockSpec((block, width), lambda i: (i, 0)),
        out_shape=jax.ShapeDtypeStruct((count, width), jnp.float32),
        interpret=INTERPRET,
    )(rows, f_hi, f_lo)


def depth_stage(rows, fz, scale_a, scale_b, depth_to_line, line_wc, line_ws):
    count, depth = rows.shape
    xdev = scale_a.shape[0]
    width = line_wc.shape[1]
    ydev = count // xdev
    block = YBLOCK * xdev
    fz_hi, fz_lo = split_outside(fz)
    q_hi, q_lo = split_outside(depth_to_line)
    whole = lambda i: (0, 0)
    return pl.pallas_call(
        depth_kernel,
        grid=(ydev // YBLOCK,),
        in_specs=[
            pl.BlockSpec((block, depth), lambda i: (i, 0)),
            pl.BlockSpec((depth, depth), whole),
            pl.BlockSpec((depth, depth), whole),
            pl.BlockSpec((xdev, depth), whole),
            pl.BlockSpec((xdev, depth), whole),
            pl.BlockSpec((depth, 2 * width), whole),
            pl.BlockSpec((depth, 2 * width), whole),
            pl.BlockSpec((xdev, width), whole),
            pl.BlockSpec((xdev, width), whole),
        ],
        out_specs=pl.BlockSpec((YBLOCK, 2 * width), lambda i: (i, 0)),
        out_shape=jax.ShapeDtypeStruct((ydev, 2 * width), jnp.float32),
        interpret=INTERPRET,
    )(rows, fz_hi, fz_lo, scale_a, scale_b, q_hi, q_lo, line_wc, line_ws)


def wave_pair(first, second, length):
    turns = jnp.mod(first[:, None] * second[None, :], length).astype(jnp.float32)
    angle = 2.0 * math.pi / length * turns
    return (jnp.cos(angle), jnp.sin(angle))


def ramp_pair(shifts, length):
    freq = jnp.arange(length, dtype=jnp.int32)
    signed = jnp.mod(freq + length // 2, length) - length // 2
    turns = jnp.mod(shifts[..., None] * signed, SUB * length).astype(jnp.float32)
    angle = 2.0 * math.pi / (SUB * length) * turns
    return (jnp.cos(angle), jnp.sin(angle))


def signed_turns(shifts, freq, length):
    signed = jnp.mod(freq + length // 2, length) - length // 2
    turns = jnp.mod(shifts[..., None] * signed, SUB * length).astype(jnp.float32)
    angle = 2.0 * math.pi / (SUB * length) * turns
    return (jnp.cos(angle), jnp.sin(angle))


def packed_forward(length):
    half = length // 2
    pos = jnp.arange(length, dtype=jnp.int32)
    freq = jnp.arange(half, dtype=jnp.int32)
    wc, ws = wave_pair(pos, freq, length)
    alt = jnp.where(pos % 2 == 0, 1.0, -1.0).astype(jnp.float32)
    im_cols = jnp.concatenate([alt[:, None], -ws[:, 1:]], axis=1)
    return jnp.concatenate([wc, im_cols], axis=1)


def packed_inverse(length):
    half = length // 2
    pos = jnp.arange(length, dtype=jnp.int32)
    freq = jnp.arange(half, dtype=jnp.int32)
    wc, ws = wave_pair(freq, pos, length)
    alt = jnp.where(pos % 2 == 0, 1.0, -1.0).astype(jnp.float32)
    weight = jnp.where(freq == 0, 1.0, 2.0).astype(jnp.float32)[:, None]
    re_rows = wc * weight
    im_rows = jnp.concatenate([alt[None, :], -2.0 * ws[1:]], axis=0)
    return jnp.concatenate([re_rows, im_rows], axis=0) / length


def packed_phase(shifts, length):
    half = length // 2
    freq = jnp.arange(half + 1, dtype=jnp.int32)
    cos_k, sin_k = signed_turns(shifts, freq, length)
    zero = jnp.zeros_like(sin_k[..., :1])
    scale_a = jnp.concatenate([cos_k[..., :half], cos_k[..., half:], cos_k[..., 1:half]], axis=-1)
    scale_b = jnp.concatenate([zero, sin_k[..., 1:half], zero, -sin_k[..., 1:half]], axis=-1)
    return scale_a, scale_b


def turn(spec, scale_a, scale_b):
    half = spec.shape[-1] // 2
    low, high = spec[..., :half], spec[..., half:]
    out_low = low * scale_a[..., :half] + high * scale_b[..., :half]
    out_high = high * scale_a[..., half:] + low * scale_b[..., half:]
    return jnp.concatenate([out_low, out_high], axis=-1)


def on_device(volume, shift_x, shift_z, mask, measured):
    zparts = lax.axis_size("zblock")
    zindex = lax.axis_index("zblock")
    yindex = lax.axis_index("yslab")
    ydev, zdev, width = volume.shape
    depth = zdev * zparts
    xdev = width // zparts
    zstart = zindex * zdev
    xstart = zindex * xdev
    tilts = shift_x.shape[0]
    scale = 1.0 / math.sqrt(depth * width)
    half = width // 2

    fx = packed_forward(width)
    gx = packed_inverse(width)
    fz = packed_forward(depth)
    gz = packed_inverse(depth)

    xfreq = jnp.arange(width, dtype=jnp.int32)
    xlocal = jnp.arange(xdev, dtype=jnp.int32) + xstart
    line_wc, line_ws = wave_pair(xlocal, xfreq, width)

    rows = volume.reshape(ydev * zdev, width)
    spec_x = forward_stage(rows, fx).reshape(ydev, zdev, width)

    partial = []
    for tilt in range(tilts):
        local_shift = lax.dynamic_slice_in_dim(shift_x[tilt], zstart, zdev, 0)
        near_a, near_b = packed_phase(local_shift, width)
        turned = turn(spec_x, near_a[None], near_b[None])
        first = forward_stage(turned.reshape(ydev * zdev, width), gx)
        first = first.reshape(ydev, zdev, width)
        columns = lax.all_to_all(first, "zblock", split_axis=2, concat_axis=1, tiled=True)
        columns = jnp.transpose(columns, (0, 2, 1))
        column_shift = lax.dynamic_slice_in_dim(shift_z[tilt], xstart, xdev, 0)
        col_a, col_b = packed_phase(column_shift, depth)
        ph_c, ph_s = ramp_pair(shift_x[tilt], width)
        depth_to_line = jnp.matmul(gz, jnp.concatenate([ph_c, ph_s], axis=1), precision=HIGH)
        mixed = depth_stage(
            columns.reshape(ydev * xdev, depth), fz, col_a, col_b, depth_to_line, line_wc, line_ws
        )
        full_re, full_im = mixed[:, :width], mixed[:, width:]
        partial.append(jnp.stack((full_re, full_im)) * scale)

    pieces = jnp.stack(partial)
    kdev = width // zparts
    pieces = pieces.reshape(tilts, 2, ydev, zparts, kdev)
    pieces = jnp.moveaxis(pieces, 3, 0)
    pieces = lax.all_to_all(pieces, "zblock", 0, 0, tiled=True)
    lines = jnp.sum(pieces, axis=0)
    spec_re = lines[:, 0]
    spec_im = lines[:, 1]
    yparts = lax.axis_size("yslab")
    rows_all = ydev * yparts
    ylocal = jnp.arange(ydev, dtype=jnp.int32) + yindex * ydev
    kfreq = jnp.arange(rows_all, dtype=jnp.int32)
    wave_cos, wave_sin = wave_pair(kfreq, ylocal, rows_all)
    term_re = jnp.einsum("ky,tyx->ktx", wave_cos, spec_re, precision=HIGH) + jnp.einsum(
        "ky,tyx->ktx", wave_sin, spec_im, precision=HIGH
    )
    term_im = jnp.einsum("ky,tyx->ktx", wave_cos, spec_im, precision=HIGH) - jnp.einsum(
        "ky,tyx->ktx", wave_sin, spec_re, precision=HIGH
    )
    terms = jnp.stack((term_re, term_im), axis=1) / math.sqrt(rows_all)
    terms = terms.reshape((yparts, ydev) + terms.shape[1:])
    terms = lax.all_to_all(terms, "yslab", 0, 0, tiled=True)
    gathered = jnp.sum(terms, axis=0)
    spectrum = jnp.transpose(gathered, (1, 2, 0, 3))
    weight = mask.astype(jnp.float32)[None]
    return spectrum + weight * (measured - spectrum)


def solution(mesh):
    in_specs = (
        P("yslab", "zblock", None),
        P(),
        P(),
        P(None, "yslab", "zblock"),
        P(None, None, "yslab", "zblock"),
    )
    out_specs = P(None, None, "yslab", "zblock")
    return jax.shard_map(
        on_device, mesh=mesh, in_specs=in_specs, out_specs=out_specs, check_vma=False
    )
```

```python
import math
import os

import jax
import jax.numpy as jnp
from jax import lax
from jax.experimental import pallas as pl
from jax.sharding import PartitionSpec as P

SUB = 64


HIGH = lax.Precision.HIGH
INTERPRET = os.environ.get("SOL_INTERPRET") == "1"
YBLOCK = 64


def split_bf16(value):
    high = value.astype(jnp.bfloat16)
    low = (value - high.astype(jnp.float32)).astype(jnp.bfloat16)
    return high, low


def split_outside(value):
    high = lax.reduce_precision(value, exponent_bits=8, mantissa_bits=7)
    return high.astype(jnp.bfloat16), (value - high).astype(jnp.bfloat16)


def dot3(lhs, rhs_high, rhs_low):
    lhs_high, lhs_low = split_bf16(lhs)
    out = jnp.dot(lhs_high, rhs_high, preferred_element_type=jnp.float32)
    out += jnp.dot(lhs_high, rhs_low, preferred_element_type=jnp.float32)
    out += jnp.dot(lhs_low, rhs_high, preferred_element_type=jnp.float32)
    return out


def depth_kernel(rows_ref, fz_hi, fz_lo, a_ref, b_ref, q_hi, q_lo, wc_ref, ws_ref, out_ref):
    xdev, depth = a_ref.shape
    half = depth // 2
    width = wc_ref.shape[1]
    spec = dot3(rows_ref[...], fz_hi[...], fz_lo[...])
    spec = spec.reshape(-1, xdev, depth)
    scale_a = a_ref[...][None]
    scale_b = b_ref[...][None]
    low, high = spec[..., :half], spec[..., half:]
    out_low = low * scale_a[..., :half] + high * scale_b[..., :half]
    out_high = high * scale_a[..., half:] + low * scale_b[..., half:]
    turned = jnp.concatenate([out_low, out_high], axis=-1).reshape(-1, depth)
    mixed = dot3(turned, q_hi[...], q_lo[...]).reshape(-1, xdev, 2 * width)
    mix_c, mix_s = mixed[..., :width], mixed[..., width:]
    wc = wc_ref[...][None]
    ws = ws_ref[...][None]
    out_ref[:, :width] = jnp.sum(wc * mix_c - ws * mix_s, axis=1)
    out_ref[:, width:] = -jnp.sum(wc * mix_s + ws * mix_c, axis=1)


def forward_kernel(rows_ref, f_hi, f_lo, out_ref):
    out_ref[...] = dot3(rows_ref[...], f_hi[...], f_lo[...])


def forward_stage(rows, matrix):
    count, width = rows.shape
    block = 256
    f_hi, f_lo = split_outside(matrix)
    whole = lambda i: (0, 0)
    return pl.pallas_call(
        forward_kernel,
        grid=(count // block,),
        in_specs=[
            pl.BlockSpec((block, width), lambda i: (i, 0)),
            pl.BlockSpec((width, width), whole),
            pl.BlockSpec((width, width), whole),
        ],
        out_specs=pl.BlockSpec((block, width), lambda i: (i, 0)),
        out_shape=jax.ShapeDtypeStruct((count, width), jnp.float32),
        interpret=INTERPRET,
    )(rows, f_hi, f_lo)


def depth_stage(rows, fz, scale_a, scale_b, depth_to_line, line_wc, line_ws):
    count, depth = rows.shape
    xdev = scale_a.shape[0]
    width = line_wc.shape[1]
    ydev = count // xdev
    block = YBLOCK * xdev
    fz_hi, fz_lo = split_outside(fz)
    q_hi, q_lo = split_outside(depth_to_line)
    whole = lambda i: (0, 0)
    return pl.pallas_call(
        depth_kernel,
        grid=(ydev // YBLOCK,),
        in_specs=[
            pl.BlockSpec((block, depth), lambda i: (i, 0)),
            pl.BlockSpec((depth, depth), whole),
            pl.BlockSpec((depth, depth), whole),
            pl.BlockSpec((xdev, depth), whole),
            pl.BlockSpec((xdev, depth), whole),
            pl.BlockSpec((depth, 2 * width), whole),
            pl.BlockSpec((depth, 2 * width), whole),
            pl.BlockSpec((xdev, width), whole),
            pl.BlockSpec((xdev, width), whole),
        ],
        out_specs=pl.BlockSpec((YBLOCK, 2 * width), lambda i: (i, 0)),
        out_shape=jax.ShapeDtypeStruct((ydev, 2 * width), jnp.float32),
        interpret=INTERPRET,
    )(rows, fz_hi, fz_lo, scale_a, scale_b, q_hi, q_lo, line_wc, line_ws)


def wave_pair(first, second, length):
    turns = jnp.mod(first[:, None] * second[None, :], length).astype(jnp.float32)
    angle = 2.0 * math.pi / length * turns
    return (jnp.cos(angle), jnp.sin(angle))


def ramp_pair(shifts, length):
    freq = jnp.arange(length, dtype=jnp.int32)
    signed = jnp.mod(freq + length // 2, length) - length // 2
    turns = jnp.mod(shifts[..., None] * signed, SUB * length).astype(jnp.float32)
    angle = 2.0 * math.pi / (SUB * length) * turns
    return (jnp.cos(angle), jnp.sin(angle))


def signed_turns(shifts, freq, length):
    signed = jnp.mod(freq + length // 2, length) - length // 2
    turns = jnp.mod(shifts[..., None] * signed, SUB * length).astype(jnp.float32)
    angle = 2.0 * math.pi / (SUB * length) * turns
    return (jnp.cos(angle), jnp.sin(angle))


def packed_forward(length):
    half = length // 2
    pos = jnp.arange(length, dtype=jnp.int32)
    freq = jnp.arange(half, dtype=jnp.int32)
    wc, ws = wave_pair(pos, freq, length)
    alt = jnp.where(pos % 2 == 0, 1.0, -1.0).astype(jnp.float32)
    im_cols = jnp.concatenate([alt[:, None], -ws[:, 1:]], axis=1)
    return jnp.concatenate([wc, im_cols], axis=1)


def packed_inverse(length):
    half = length // 2
    pos = jnp.arange(length, dtype=jnp.int32)
    freq = jnp.arange(half, dtype=jnp.int32)
    wc, ws = wave_pair(freq, pos, length)
    alt = jnp.where(pos % 2 == 0, 1.0, -1.0).astype(jnp.float32)
    weight = jnp.where(freq == 0, 1.0, 2.0).astype(jnp.float32)[:, None]
    re_rows = wc * weight
    im_rows = jnp.concatenate([alt[None, :], -2.0 * ws[1:]], axis=0)
    return jnp.concatenate([re_rows, im_rows], axis=0) / length


def packed_phase(shifts, length):
    half = length // 2
    freq = jnp.arange(half + 1, dtype=jnp.int32)
    cos_k, sin_k = signed_turns(shifts, freq, length)
    zero = jnp.zeros_like(sin_k[..., :1])
    scale_a = jnp.concatenate([cos_k[..., :half], cos_k[..., half:], cos_k[..., 1:half]], axis=-1)
    scale_b = jnp.concatenate([zero, sin_k[..., 1:half], zero, -sin_k[..., 1:half]], axis=-1)
    return scale_a, scale_b


def turn(spec, scale_a, scale_b):
    half = spec.shape[-1] // 2
    low, high = spec[..., :half], spec[..., half:]
    out_low = low * scale_a[..., :half] + high * scale_b[..., :half]
    out_high = high * scale_a[..., half:] + low * scale_b[..., half:]
    return jnp.concatenate([out_low, out_high], axis=-1)


def on_device(volume, shift_x, shift_z, mask, measured):
    zparts = lax.axis_size("zblock")
    zindex = lax.axis_index("zblock")
    yindex = lax.axis_index("yslab")
    ydev, zdev, width = volume.shape
    depth = zdev * zparts
    xdev = width // zparts
    zstart = zindex * zdev
    xstart = zindex * xdev
    tilts = shift_x.shape[0]
    scale = 1.0 / math.sqrt(depth * width)
    half = width // 2

    fx = packed_forward(width)
    gx = packed_inverse(width)
    fz = packed_forward(depth)
    gz = packed_inverse(depth)

    xfreq = jnp.arange(width, dtype=jnp.int32)
    xlocal = jnp.arange(xdev, dtype=jnp.int32) + xstart
    line_wc, line_ws = wave_pair(xlocal, xfreq, width)

    rows = volume.reshape(ydev * zdev, width)
    spec_x = forward_stage(rows, fx).reshape(ydev, zdev, width)

    partial = []
    for tilt in range(tilts):
        local_shift = lax.dynamic_slice_in_dim(shift_x[tilt], zstart, zdev, 0)
        near_a, near_b = packed_phase(local_shift, width)
        turned = turn(spec_x, near_a[None], near_b[None])
        first = jnp.matmul(turned.reshape(ydev * zdev, width), gx, precision=HIGH)
        first = first.reshape(ydev, zdev, width)
        columns = lax.all_to_all(first, "zblock", split_axis=2, concat_axis=1, tiled=True)
        columns = jnp.transpose(columns, (0, 2, 1))
        column_shift = lax.dynamic_slice_in_dim(shift_z[tilt], xstart, xdev, 0)
        col_a, col_b = packed_phase(column_shift, depth)
        ph_c, ph_s = ramp_pair(shift_x[tilt], width)
        depth_to_line = jnp.matmul(gz, jnp.concatenate([ph_c, ph_s], axis=1), precision=HIGH)
        mixed = depth_stage(
            columns.reshape(ydev * xdev, depth), fz, col_a, col_b, depth_to_line, line_wc, line_ws
        )
        full_re, full_im = mixed[:, :width], mixed[:, width:]
        partial.append(jnp.stack((full_re, full_im)) * scale)

    pieces = jnp.stack(partial)
    kdev = width // zparts
    pieces = pieces.reshape(tilts, 2, ydev, zparts, kdev)
    pieces = jnp.moveaxis(pieces, 3, 0)
    pieces = lax.all_to_all(pieces, "zblock", 0, 0, tiled=True)
    lines = jnp.sum(pieces, axis=0)
    spec_re = lines[:, 0]
    spec_im = lines[:, 1]
    yparts = lax.axis_size("yslab")
    rows_all = ydev * yparts
    ylocal = jnp.arange(ydev, dtype=jnp.int32) + yindex * ydev
    kfreq = jnp.arange(rows_all, dtype=jnp.int32)
    wave_cos, wave_sin = wave_pair(kfreq, ylocal, rows_all)
    term_re = jnp.einsum("ky,tyx->ktx", wave_cos, spec_re, precision=HIGH) + jnp.einsum(
        "ky,tyx->ktx", wave_sin, spec_im, precision=HIGH
    )
    term_im = jnp.einsum("ky,tyx->ktx", wave_cos, spec_im, precision=HIGH) - jnp.einsum(
        "ky,tyx->ktx", wave_sin, spec_re, precision=HIGH
    )
    terms = jnp.stack((term_re, term_im), axis=1) / math.sqrt(rows_all)
    terms = terms.reshape((yparts, ydev) + terms.shape[1:])
    terms = lax.all_to_all(terms, "yslab", 0, 0, tiled=True)
    gathered = jnp.sum(terms, axis=0)
    spectrum = jnp.transpose(gathered, (1, 2, 0, 3))
    weight = mask.astype(jnp.float32)[None]
    return spectrum + weight * (measured - spectrum)


def solution(mesh):
    in_specs = (
        P("yslab", "zblock", None),
        P(),
        P(),
        P(None, "yslab", "zblock"),
        P(None, None, "yslab", "zblock"),
    )
    out_specs = P(None, None, "yslab", "zblock")
    return jax.shard_map(
        on_device, mesh=mesh, in_specs=in_specs, out_specs=out_specs, check_vma=False
    )
```
